32 devices in a mesh: dp: 2 (over x), space: 16 (over z, y, core).
Axes of the slice: x: 2, y: 2, z: 4, core: 2. Of those that a mesh axis runs over, the one named last changes fastest.
Arguments:
- volumes: bfloat16 [2, 4, 128, 128, 128], P('dp', None, 'space'), may hold values from -6 to 6
- kernel_one: bfloat16 [16, 4, 3, 3, 3], replicated, may hold values from -0.625 to 0.625
- kernel_two: bfloat16 [32, 16, 3, 3, 3], replicated, may hold values from -0.3125 to 0.3125
- cotangent: bfloat16 [2, 32, 32, 1024], P('dp', None, None, 'space'), may hold values from -6 to 6
Outputs:
- output_two: bfloat16 [2, 32, 32, 1024], P('dp', None, None, 'space')
- grad_one: float32 [16, 4, 3, 3, 3], replicated
- grad_two: float32 [32, 16, 3, 3, 3], replicated
The draws below stay inside these ranges and needn't reach their ends.
All inputs are finite; a program needn't handle non-finite values.
Results may differ from the reference program's by a relative error of at most 0.004.
The reference program's roundings to bfloat16 on the way (of `hidden_one`, `delta_two` and `delta_one`) count: a program that leaves them out, or rounds other values in their place, can miss the bound.
Values may be sent and summed in bfloat16 or wider, within the bound.
No kernel may reach another device: no remote copies, remote signals or barrier semaphores. Data moves between devices by JAX's collectives and lax.ppermute only.
A program may use at most 256 MiB of HBM per device.

```python
import jax
import jax.numpy as jnp
from jax import lax

CIN = 4
C1 = 16
C2 = 32
SIDE = 128
PLANE = 128
VOLS = 2


def block_scale(own_key, extent, cuts, least, top_value):
    def one(dim, shards_of):
        steps = jax.random.uniform(jax.random.fold_in(jax.random.fold_in(own_key, 6), dim), (shards_of,), jnp.float32, least / len(cuts), top_value / len(cuts))
        return jnp.repeat(jnp.exp(steps), extent[dim] // shards_of).reshape((-1,) + (1,) * (len(extent) - dim - 1))

    factor_of = one(*cuts[0])
    for cut in cuts[1:]:
        factor_of = factor_of * one(*cut)
    return factor_of


def centred(key, shape, spread, most, split=(), dtype=jnp.bfloat16):
    level = block_scale(key, shape, split, -0.22, 0.18) if split else 1.0
    values = jax.random.normal(key, shape, jnp.float32) * spread * level
    return jnp.minimum(jnp.maximum(values, -most), most).astype(dtype)


def setup_inputs(seed: int = 0) -> dict:
    arg_keys = jax.random.split(jax.random.key(seed), 5)
    volumes = centred(arg_keys[0], (VOLS, CIN, SIDE, PLANE, PLANE), 1.0, 6.0, ((0, 2), (2, 16)))
    kernel_one = centred(arg_keys[1], (C1, CIN, 3, 3, 3), (CIN * 27) ** -0.5, 0.625)
    kernel_two = centred(arg_keys[2], (C2, C1, 3, 3, 3), (C1 * 27) ** -0.5, 0.3125)
    cotangent = centred(arg_keys[3], (VOLS, C2, SIDE // 4, (PLANE // 4) * (PLANE // 4)), 1.0, 6.0, ((0, 2), (3, 16)))
    return dict(volumes=volumes, kernel_one=kernel_one, kernel_two=kernel_two, cotangent=cotangent)


negative_slope = 0.3

def leaky(values):
    return jnp.where(values > 0, values, negative_slope * values)

def slope_of(values):
    return jnp.where(values > 0, 1.0, negative_slope)

def rounded(values):
    return lax.optimization_barrier(values.astype(jnp.bfloat16)).astype(jnp.float32)

def strided(signal, kernel):
    return lax.conv_general_dilated(signal, kernel, (2, 2, 2), ((1, 1), (1, 1), (1, 1)), dimension_numbers=('NCDHW', 'OIDHW', 'NCDHW'), precision=lax.Precision.HIGHEST)

def reference(volumes, kernel_one, kernel_two, cotangent):
    weight_one = kernel_one.astype(jnp.float32)
    weight_two = kernel_two.astype(jnp.float32)

    def one_volume(carry, inputs):
        volume, upstream = inputs
        signal = volume.astype(jnp.float32)[None]
        linear_one = strided(signal, weight_one)
        hidden_one = rounded(leaky(linear_one))
        linear_two, pull_two = jax.vjp(lambda source, weight: strided(source, weight), hidden_one, weight_two)
        output_two = leaky(linear_two).astype(jnp.bfloat16)
        delta_two = rounded(upstream.astype(jnp.float32).reshape(linear_two.shape) * slope_of(linear_two))
        back_one, term_two = pull_two(delta_two)
        delta_one = rounded(back_one * slope_of(hidden_one))
        unused, pull_one = jax.vjp(lambda weight: strided(signal, weight), weight_one)
        term_one = pull_one(delta_one)[0]
        shaped = output_two[0].reshape(output_two.shape[1], output_two.shape[2], -1)
        return ((carry[0] + term_one, carry[1] + term_two), shaped)
    start = (jnp.zeros(kernel_one.shape, jnp.float32), jnp.zeros(kernel_two.shape, jnp.float32))
    sums, outputs = lax.scan(one_volume, start, (volumes, cotangent))
    count = volumes.shape[0] * (volumes.shape[2] // 4) * (volumes.shape[3] // 4) * (volumes.shape[4] // 4)
    factor = 1.0 / jnp.sqrt(jnp.float32(count))
    return (outputs, sums[0] * factor, sums[1] * factor)
```

```python
import functools
import math

import jax
import jax.numpy as jnp
from jax import lax
from jax.experimental import pallas as pl
from jax.experimental.pallas import tpu as pltpu
from jax.sharding import PartitionSpec as P

f32 = jnp.float32
bf16 = jnp.bfloat16

SLOPE = 0.3
BLOCKS = 4
HB = 32
CIN, C1, C2 = 4, 16, 32
W0, W1, W2 = 32, 16, 8
ROWS = BLOCKS * HB
LA, LH, LZ = W0 * CIN, W1 * C1, W2 * C2
WIDE = BLOCKS * LZ
TAPS = [(kd, kh) for kd in range(3) for kh in range(3)]
INPUT_ROWS = {(0, 0): 4, (0, 1): 0, (0, 2): 1, (1, 0): 1, (1, 1): 2, (1, 2): 3}


def dot(a, b):
    return jnp.dot(a, b, preferred_element_type=f32)


def dot_nt(a, b):
    return lax.dot_general(a, b, (((1,), (1,)), ((), ())), preferred_element_type=f32)


def dot_tn(a, b):
    return lax.dot_general(a, b, (((0,), (0,)), ((), ())), preferred_element_type=f32)


def exact_nt(a, b):
    return lax.dot_general(
        a, b, (((1,), (1,)), ((), ())), precision=lax.Precision.HIGHEST, preferred_element_type=f32
    )


def iotas(shape):
    return lax.broadcasted_iota(jnp.int32, shape, 0), lax.broadcasted_iota(jnp.int32, shape, 1)


def one_hot(mask):
    return jnp.where(mask, 1.0, 0.0).astype(bf16)


def width_order():
    r, q = iotas((CIN * 128, CIN * 128))
    return one_hot(r == (q % CIN) * 128 + (q // LA) * W0 + (q // CIN) % W0)


def height_order():
    r, q = iotas((5 * HB, 4 * HB))
    return one_hot(q == 4 * (r % HB) + jnp.where(r // HB == 4, -1, r // HB))


def channel_order():
    r, q = iotas((WIDE, WIDE))
    cells = BLOCKS * W2
    return one_hot(r == (q % cells) * C2 + q // cells)


def arrange_planes(planes, count, put):
    x = jnp.concatenate([planes(c) for c in range(CIN)], axis=1)
    y = dot(x, width_order()).astype(bf16)
    order = height_order()
    none = jnp.zeros((HB, LA), bf16)
    for d in range(count):
        z = dot(order, y[d * 128 : (d + 1) * 128]).astype(bf16)
        for v in range(5):
            here = [z[v * HB : (v + 1) * HB, b * LA : (b + 1) * LA] for b in range(BLOCKS)]
            own = jnp.concatenate(here, axis=0)
            before = jnp.concatenate([none] + here[:-1], axis=0)
            put(d, v, own, before)


def band(taps, rows, cin, cols, cout, put):
    r, q = iotas((rows, cols))
    w, o = r // cin, q // cout
    rel = w - 2 * o + 1
    last = (w == rows // cin - 1) & (o == 0)
    for tap in range(9):
        e = [taps(3 * tap + kw) for kw in range(3)]
        own = jnp.where(rel == 0, e[0], jnp.where(rel == 1, e[1], jnp.where(rel == 2, e[2], 0.0)))
        put(tap, own.astype(bf16), jnp.where(last, e[0], 0.0).astype(bf16))


def band_back(taps, rows, cout, cols, cin, put):
    r, q = iotas((rows, cols))
    w, o = q // cin, r // cout
    rel = w - 2 * o + 1
    last = (w == cols // cin - 1) & (o == 0)
    for tap in range(9):
        e = [taps(3 * tap + kw) for kw in range(3)]
        own = jnp.where(rel == 0, e[0], jnp.where(rel == 1, e[1], jnp.where(rel == 2, e[2], 0.0)))
        put(tap, own.astype(bf16), jnp.where(last, e[0], 0.0).astype(bf16))


def spread(k, cols):
    c, q = iotas((k.shape[1], cols))
    return dot(k, one_hot(q % k.shape[1] == c))


def prepare_kernel(vol_ref, k1_ref, k2_ref, k2t_ref, a_ref, t1_ref, t2_ref, t2b_ref, order_ref):
    count = a_ref.shape[0]

    def put_a(d, v, own, before):
        a_ref[d, v, :, :LA] = own
        a_ref[d, v, :, LA:] = before

    arrange_planes(lambda c: vol_ref[c].reshape(count * 128, 128), count, put_a)

    def puts(ref, half):
        def put(tap, own, other):
            ref[2 * half * tap : 2 * half * tap + half] = own
            ref[2 * half * tap + half : 2 * half * (tap + 1)] = other

        return put

    def tiled(k, each, times):
        return lambda t: jnp.concatenate([k[each * t : each * (t + 1)]] * times, axis=0)

    band(tiled(spread(k1_ref[...], LH), 16, LA // 16), LA, CIN, LH, C1, puts(t1_ref, LA))
    band(tiled(spread(k2_ref[...], LZ), C1, W1), LH, C1, LZ, C2, puts(t2_ref, LH))
    band_back(tiled(spread(k2t_ref[...], LH), C2, W2), LZ, C2, LH, C1, puts(t2b_ref, LZ))
    order_ref[...] = channel_order()


def shifted_down(x, keep):
    return jnp.where(keep, pltpu.roll(x.astype(f32), 1, 0), 0.0).astype(bf16)


def row_choice(d2, hl, depth):
    r, q = iotas((d2 * HB, hl * depth))
    plane, h2 = r // HB, r % HB
    return one_hot(q == (h2 % hl) * depth + (h2 // hl) * d2 + plane)


def forward_kernel(low_ref, a_ref, t1_ref, t2_ref, order_ref, cot_ref, alow_ref, hh_ref, send_ref, delta_ref):
    planes = hh_ref.shape[0]
    d2n = delta_ref.shape[0]
    depth = cot_ref.shape[0]
    hl = cot_ref.shape[1] // WIDE

    def put_a(d, v, own, before):
        alow_ref[d, v, :, :LA] = own
        alow_ref[d, v, :, LA:] = before

    arrange_planes(lambda c: low_ref[c].reshape(3 * 128, 128), 3, put_a)

    def rows_of(plane, v):
        return alow_ref[plane, v] if plane < 3 else a_ref[plane - 3, v]

    r, _ = iotas((planes * ROWS, LH))
    keep = r % HB != 0
    none = jnp.zeros((HB, LH), bf16)
    for p in range(2):
        cols = [
            jnp.concatenate([rows_of(2 * j + kd, INPUT_ROWS[p, kh]) for j in range(planes)], axis=0)
            for kd, kh in TAPS
        ]
        linear = dot(jnp.concatenate(cols, axis=1), t1_ref[...])
        hidden = jnp.where(linear > 0, linear, SLOPE * linear).astype(bf16)
        variants = [(1, hidden)] if p == 0 else [(2, hidden), (0, shifted_down(hidden, keep))]
        for v, x in variants:
            for j in range(planes):
                own = x[j * ROWS : (j + 1) * ROWS]
                hh_ref[j, v, :, :LH] = own
                hh_ref[j, v, :, LH:] = jnp.concatenate([none, own[:-HB]], axis=0)

    cols = [jnp.concatenate([hh_ref[2 * d + kd, kh] for d in range(d2n)], axis=0) for kd, kh in TAPS]
    linear = dot(jnp.concatenate(cols, axis=1), t2_ref[...])
    out = jnp.where(linear > 0, linear, SLOPE * linear).astype(bf16)

    def wide(x):
        return jnp.concatenate(
            [
                jnp.concatenate([x[d * ROWS + b * HB : d * ROWS + (b + 1) * HB] for b in range(BLOCKS)], axis=1)
                for d in range(d2n)
            ],
            axis=0,
        )

    choice = row_choice(d2n, hl, depth)
    by_channel = dot(wide(out), order_ref[...]).astype(bf16)
    sent = dot_tn(choice, by_channel).astype(bf16)
    for h in range(hl):
        send_ref[:, h * WIDE : (h + 1) * WIDE] = sent[h * depth : (h + 1) * depth]

    got = jnp.concatenate([cot_ref[:, h * WIDE : (h + 1) * WIDE] for h in range(hl)], axis=0)
    chosen = dot(choice, got).astype(bf16)
    cot = dot_nt(chosen, order_ref[...])
    for d in range(d2n):
        for b in range(BLOCKS):
            z = linear[d * ROWS + b * HB : d * ROWS + (b + 1) * HB]
            c = cot[d * HB : (d + 1) * HB, b * LZ : (b + 1) * LZ]
            delta_ref[d, b * HB : (b + 1) * HB] = (c * jnp.where(z > 0, 1.0, SLOPE)).astype(bf16)


def diagonals(g, first, cells, cout, cin):
    lanes = 2 * cells * cin
    _, q = iotas((cout, lanes))
    w = q // cin
    ahead = jnp.zeros((cout, lanes), f32)
    behind = jnp.where(w == 2 * cells - 1, g[:cout, first + lanes : first + 2 * lanes], 0.0)
    for o in range(cells):
        x = g[o * cout : (o + 1) * cout, first : first + lanes]
        ahead = jnp.where(w // 2 == o, x, ahead)
        if o:
            behind = jnp.where(w == 2 * o - 1, x, behind)
    return ahead, behind


def width_sums(g, cells, cout, cin):
    lanes = 2 * cells * cin
    both = [diagonals(g, 2 * lanes * tap, cells, cout, cin) for tap in range(9)]
    ahead = jnp.concatenate([x for x, _ in both], axis=0)
    behind = jnp.concatenate([x for _, x in both], axis=0)
    r, q = iotas((2 * cin, lanes))
    pick = jnp.where((q // cin % 2 == r // cin) & (q % cin == r % cin), 1.0, 0.0)
    pad = max(cin, 8)
    r, q = iotas((pad, lanes))
    every = jnp.where(q % cin == r, 1.0, 0.0)
    return exact_nt(pick, ahead), exact_nt(every, behind)


def second_gradient_kernel(hh_ref, delta_ref, out_ref):
    d2n = delta_ref.shape[0]
    delta = jnp.concatenate([delta_ref[d] for d in range(d2n)], axis=0)
    cols = [jnp.concatenate([hh_ref[2 * d + kd, kh] for d in range(d2n)], axis=0) for kd, kh in TAPS]
    g = dot_tn(delta, jnp.concatenate(cols, axis=1))
    ahead, behind = width_sums(g, W2, C2, C1)
    out_ref[: 2 * C1] = ahead
    out_ref[2 * C1 :] = behind


def first_gradient_kernel(hh_ref, delta_ref, next_ref, t2b_ref, alow_ref, a_ref, out_ref, dv_ref):
    d2n = delta_ref.shape[0]
    d1n = 2 * d2n
    r, _ = iotas((ROWS, LZ))
    keep = r % HB != HB - 1
    none = jnp.zeros((HB, LZ), bf16)
    for d in range(d2n + 1):
        x = delta_ref[d] if d < d2n else next_ref[...]
        up = jnp.where(keep, pltpu.roll(x.astype(f32), ROWS - 1, 0), 0.0).astype(bf16)
        for v, y in enumerate((x, up)):
            dv_ref[d, v, :, :LZ] = y
            dv_ref[d, v, :, LZ:] = jnp.concatenate([y[HB:], none], axis=0)

    def pulled(first, kd, kh):
        v = 1 if kh == 0 else 0
        lhs = jnp.concatenate([dv_ref[d + first, v] for d in range(d2n)], axis=0)
        tap = 3 * kd + kh
        return lhs, t2b_ref[2 * LZ * tap : 2 * LZ * (tap + 1)]

    def rows_of(plane, v):
        return alow_ref[plane, v] if plane < 3 else a_ref[plane - 3, v]

    deltas, cols = [], []
    for p in range(2):
        heights = (1,) if p == 0 else (2, 0)
        for even in range(2):
            depths = ((0, 2), (1, 0)) if even else ((0, 1),)
            terms = [pulled(first, kd, kh) for first, kd in depths for kh in heights]
            back = dot(
                jnp.concatenate([lhs for lhs, _ in terms], axis=1),
                jnp.concatenate([rhs for _, rhs in terms], axis=0),
            )
            planes = [2 * d + 1 + even for d in range(d2n)]
            hidden = jnp.concatenate([hh_ref[j, 2 if p else 1, :, :LH] for j in planes], axis=0)
            deltas.append((back * jnp.where(hidden.astype(f32) > 0, 1.0, SLOPE)).astype(bf16))
            cols.append(
                jnp.concatenate(
                    [
                        jnp.concatenate([rows_of(2 * j + kd, INPUT_ROWS[p, kh]) for j in planes], axis=0)
                        for kd, kh in TAPS
                    ],
                    axis=1,
                )
            )
    g = dot_tn(jnp.concatenate(deltas, axis=0), jnp.concatenate(cols, axis=0))
    ahead, behind = width_sums(g, W1, C1, CIN)
    out_ref[: 2 * CIN] = ahead
    out_ref[2 * CIN :] = behind


def gather_kernel(cot_ref, out_ref):
    channels, depth, cells = cot_ref.shape
    hl = cells // 32
    r, q = iotas((cells, hl * 128))
    for first in range(0, channels, 4):
        total = None
        for i in range(4):
            move = one_hot((q // 128 == r // 32) & (q % 128 == i * 32 + r % 32))
            part = dot(cot_ref[first + i], move)
            total = part if total is None else total + part
        for h in range(hl):
            at = h * WIDE + first * 32
            out_ref[:, at : at + 128] = total[:, h * 128 : (h + 1) * 128].astype(bf16)


def scatter_kernel(got_ref, out_ref):
    channels, depth, cells = out_ref.shape
    hl = cells // 32
    r, q = iotas((hl * 128, cells))
    for first in range(0, channels, 4):
        x = jnp.concatenate(
            [got_ref[:, h * WIDE + first * 32 : h * WIDE + first * 32 + 128] for h in range(hl)], axis=1
        )
        for i in range(4):
            move = one_hot((r // 128 == q // 32) & (r % 128 == i * 32 + q % 32))
            out_ref[first + i] = dot(x, move).astype(bf16)


def call(kernel, name, outs, *args, scratch=()):
    return pl.pallas_call(
        kernel,
        name=name,
        out_shape=[jax.ShapeDtypeStruct(shape, dtype) for shape, dtype in outs],
        scratch_shapes=list(scratch),
        compiler_params=pltpu.CompilerParams(vmem_limit_bytes=56 << 20),
    )(*args)


def passed_along(block, distance):
    devices = range(lax.axis_size("space"))
    return lax.ppermute(block, "space", [(i - distance, i) for i in devices if i - distance in devices])


def total_of(terms):
    count = lax.axis_size("dp") * lax.axis_size("space")
    step = 1
    while step < count:
        terms = terms + lax.ppermute(terms, ("dp", "space"), [(i, i ^ step) for i in range(count)])
        step *= 2
    return terms


def exchanged(rows):
    depth, lanes = rows.shape
    devices = lax.axis_size("space")
    blocks = rows.reshape(devices, depth // devices, lanes)
    return lax.all_to_all(blocks, "space", 0, 0, tiled=True).reshape(depth, lanes)


def local(volumes, kernel_one, kernel_two, cotangent):
    _, _, planes, height, _ = volumes.shape
    d1n, d2n = planes // 2, planes // 4
    _, _, depth, cells = cotangent.shape
    vol, cot = volumes[0], cotangent[0]

    low = passed_along(vol[:, -3:], 1)
    (cot_rows,) = call(gather_kernel, "gather", [((depth, cells * C2), bf16)], cot)
    cot_here = exchanged(cot_rows)

    k1 = kernel_one.transpose(2, 3, 4, 1, 0).reshape(27, 1, CIN, C1)
    k1 = jnp.broadcast_to(k1, (27, 16 // CIN, CIN, C1)).reshape(27 * 16, C1)
    k2 = kernel_two.transpose(2, 3, 4, 1, 0).reshape(27 * C1, C2)
    k2t = kernel_two.transpose(2, 3, 4, 0, 1).reshape(27 * C2, C1)
    a, t1, t2, t2b, order = call(
        prepare_kernel,
        "prepare",
        [
            ((planes, 5, ROWS, 2 * LA), bf16),
            ((9 * 2 * LA, LH), bf16),
            ((9 * 2 * LH, LZ), bf16),
            ((9 * 2 * LZ, LH), bf16),
            ((WIDE, WIDE), bf16),
        ],
        vol,
        k1,
        k2,
        k2t,
    )
    a_low, hh, send, delta = call(
        forward_kernel,
        "forward",
        [
            ((3, 5, ROWS, 2 * LA), bf16),
            ((d1n + 1, 3, ROWS, 2 * LH), bf16),
            ((depth, cells * C2), bf16),
            ((d2n, ROWS, LZ), bf16),
        ],
        low,
        a,
        t1,
        t2,
        order,
        cot_here,
    )
    delta_next = passed_along(delta[0], -1)
    got = exchanged(send)
    (term_two,) = call(second_gradient_kernel, "second_gradient", [((3 * C1, 9 * C2), f32)], hh, delta)
    (term_one,) = call(
        first_gradient_kernel,
        "first_gradient",
        [((16, 9 * C1), f32)],
        hh,
        delta,
        delta_next,
        t2b,
        a_low,
        a,
        scratch=[pltpu.VMEM((d2n + 1, 2, ROWS, 2 * LZ), bf16)],
    )
    terms = jnp.concatenate([term_two, jnp.pad(term_one, ((0, 0), (0, 9 * (C2 - C1))))], axis=0)
    (out,) = call(scatter_kernel, "scatter", [((C2, depth, cells), bf16)], got)
    totals = total_of(terms)

    count = volumes.shape[0] * lax.axis_size("dp")
    factor = 1.0 / math.sqrt(count * depth * (height // 4) ** 2)
    two = jnp.roll(totals[: 3 * C1].reshape(3, C1, 3, 3, C2), 1, axis=0) * factor
    one = totals[3 * C1 : 3 * C1 + 3 * CIN, : 9 * C1].reshape(3, CIN, 3, 3, C1)
    one = jnp.roll(one, 1, axis=0) * factor
    return (
        out[None],
        one.transpose(4, 1, 2, 3, 0),
        two.transpose(4, 1, 2, 3, 0),
    )


def solution(mesh):
    placed = (P("dp", None, "space", None, None), P(), P(), P("dp", None, None, "space"))
    return jax.shard_map(
        local,
        mesh=mesh,
        in_specs=placed,
        out_specs=(P("dp", None, None, "space"), P(), P()),
        check_vma=False,
    )
```

```python
import functools
import math

import jax
import jax.numpy as jnp
from jax import lax
from jax.experimental import pallas as pl
from jax.experimental.pallas import tpu as pltpu
from jax.sharding import PartitionSpec as P

f32 = jnp.float32
bf16 = jnp.bfloat16

SLOPE = 0.3
BLOCKS = 4
HB = 32
CIN, C1, C2 = 4, 16, 32
W0, W1, W2 = 32, 16, 8
ROWS = BLOCKS * HB
LA, LH, LZ = W0 * CIN, W1 * C1, W2 * C2
WIDE = BLOCKS * LZ
TAPS = [(kd, kh) for kd in range(3) for kh in range(3)]
INPUT_ROWS = {(0, 0): 4, (0, 1): 0, (0, 2): 1, (1, 0): 1, (1, 1): 2, (1, 2): 3}


def dot(a, b):
    return jnp.dot(a, b, preferred_element_type=f32)


def dot_nt(a, b):
    return lax.dot_general(a, b, (((1,), (1,)), ((), ())), preferred_element_type=f32)


def dot_tn(a, b):
    return lax.dot_general(a, b, (((0,), (0,)), ((), ())), preferred_element_type=f32)


def exact_nt(a, b):
    return lax.dot_general(
        a, b, (((1,), (1,)), ((), ())), precision=lax.Precision.HIGHEST, preferred_element_type=f32
    )


def iotas(shape):
    return lax.broadcasted_iota(jnp.int32, shape, 0), lax.broadcasted_iota(jnp.int32, shape, 1)


def one_hot(mask):
    return jnp.where(mask, 1.0, 0.0).astype(bf16)


def width_order():
    r, q = iotas((CIN * 128, CIN * 128))
    return one_hot(r == (q % CIN) * 128 + (q // LA) * W0 + (q // CIN) % W0)


def height_order():
    r, q = iotas((5 * HB, 4 * HB))
    return one_hot(q == 4 * (r % HB) + jnp.where(r // HB == 4, -1, r // HB))


def channel_order():
    r, q = iotas((WIDE, WIDE))
    cells = BLOCKS * W2
    return one_hot(r == (q % cells) * C2 + q // cells)


def arrange_planes(planes, count, put):
    x = jnp.concatenate([planes(c) for c in range(CIN)], axis=1)
    y = dot(x, width_order()).astype(bf16)
    order = height_order()
    for d in range(count):
        z = dot(order, y[d * 128 : (d + 1) * 128]).astype(bf16)
        for v in range(5):
            put(d, v, [z[v * HB : (v + 1) * HB, b * LA : (b + 1) * LA] for b in range(BLOCKS)])


def with_before(x):
    return jnp.concatenate([x, jnp.concatenate([jnp.zeros_like(x[:HB]), x[:-HB]], axis=0)], axis=1)


def band(taps, rows, cin, cols, cout, put):
    r, q = iotas((rows, cols))
    w, o = r // cin, q // cout
    rel = w - 2 * o + 1
    last = (w == rows // cin - 1) & (o == 0)
    for tap in range(9):
        e = [taps(3 * tap + kw) for kw in range(3)]
        own = jnp.where(rel == 0, e[0], jnp.where(rel == 1, e[1], jnp.where(rel == 2, e[2], 0.0)))
        put(tap, own.astype(bf16), jnp.where(last, e[0], 0.0).astype(bf16))


def band_back(taps, rows, cout, cols, cin, put):
    r, q = iotas((rows, cols))
    w, o = q // cin, r // cout
    rel = w - 2 * o + 1
    last = (w == cols // cin - 1) & (o == 0)
    for tap in range(9):
        e = [taps(3 * tap + kw) for kw in range(3)]
        own = jnp.where(rel == 0, e[0], jnp.where(rel == 1, e[1], jnp.where(rel == 2, e[2], 0.0)))
        put(tap, own.astype(bf16), jnp.where(last, e[0], 0.0).astype(bf16))


def spread(k, cols):
    c, q = iotas((k.shape[1], cols))
    return dot(k, one_hot(q % k.shape[1] == c))


def spread_back(k2):
    r, q = iotas((C2, C2))
    flipped = dot_nt(one_hot(r == q), k2).astype(bf16)
    flipped = jnp.concatenate([flipped, jnp.zeros((C2, 512 - 27 * C1), bf16)], axis=1)
    stacked = jnp.concatenate([flipped[:, 128 * i : 128 * (i + 1)] for i in range(4)], axis=0)
    r, q = iotas((128, LH))
    parts = [dot(stacked, one_hot((r // C1 == g) & (q % C1 == r % C1))) for g in range(8)]
    return lambda t: parts[t % 8][C2 * (t // 8) : C2 * (t // 8 + 1)]


def shifted_down(x, keep):
    return jnp.where(keep, pltpu.roll(x.astype(f32), 1, 0), 0.0).astype(bf16)


def travel_order(r, depth, d2n, hl):
    groups = hl * C2 // 4
    return (r // d2n) % groups, r // (groups * d2n) * d2n + r % d2n


def by_height(r, d2n):
    group, plane, h2 = r // (d2n * HB), (r // HB) % d2n, r % HB
    return (h2 * (C2 // 4) + group) * d2n + plane


def puts(ref, half):
    def put(tap, own, other):
        ref[2 * half * tap : 2 * half * tap + half] = own
        ref[2 * half * tap + half : 2 * half * (tap + 1)] = other

    return put


def tiled(each, times):
    return lambda t: jnp.concatenate([each(t)] * times, axis=0)


def forward_kernel(
    vol_ref, low_ref, k1_ref, k2_ref, order_ref, a_ref, hh_ref, send_ref, slope_ref, own_ref, t1_ref, t2_ref, sem
):
    count = vol_ref.shape[1]
    planes = hh_ref.shape[0]
    d2n = slope_ref.shape[0]
    copy = pltpu.make_async_copy(vol_ref, own_ref, sem)
    copy.start()

    def put_from(first):
        def put(d, v, blocks):
            for b, x in enumerate(blocks):
                a_ref[first + d, v, b * HB : (b + 1) * HB] = x

        return put

    arrange_planes(lambda c: low_ref[c].reshape(3 * 128, 128), 3, put_from(0))
    k1 = jnp.concatenate([k1_ref[t].astype(f32) for t in range(27) for _ in range(16 // CIN)], axis=0)
    k1 = spread(k1.astype(bf16), LH)
    band(tiled(lambda t: k1[16 * t : 16 * (t + 1)], LA // 16), LA, CIN, LH, C1, puts(t1_ref, LA))
    k2 = spread(k2_ref[...], LZ)
    band(tiled(lambda t: k2[C1 * t : C1 * (t + 1)], W1), LH, C1, LZ, C2, puts(t2_ref, LH))
    copy.wait()
    arrange_planes(lambda c: own_ref[c].reshape(count * 128, 128), count, put_from(3))

    r, _ = iotas((planes * ROWS, LH))
    keep = r % HB != 0
    for p in range(2):
        cols = [
            jnp.concatenate([with_before(a_ref[2 * j + kd, INPUT_ROWS[p, kh]]) for j in range(planes)], axis=0)
            for kd, kh in TAPS
        ]
        linear = dot(jnp.concatenate(cols, axis=1), t1_ref[...])
        hidden = jnp.where(linear > 0, linear, SLOPE * linear).astype(bf16)
        variants = [(1, hidden)] if p == 0 else [(2, hidden), (0, shifted_down(hidden, keep))]
        for v, x in variants:
            for j in range(planes):
                hh_ref[j, v] = x[j * ROWS : (j + 1) * ROWS]

    linear = dot(second_layer_columns(hh_ref, d2n), t2_ref[...])
    out = jnp.where(linear > 0, linear, SLOPE * linear).astype(bf16)
    positive = jnp.where(linear > 0, 1.0, 0.0).astype(bf16)
    for d in range(d2n):
        slope_ref[d] = positive[d * ROWS : (d + 1) * ROWS]
    wide = jnp.concatenate(
        [
            jnp.concatenate([out[d * ROWS + b * HB : d * ROWS + (b + 1) * HB] for b in range(BLOCKS)], axis=1)
            for d in range(d2n)
        ],
        axis=0,
    )
    groups = C2 // 4
    by_channel = dot(wide, order_ref[...]).astype(bf16)
    stacked = jnp.concatenate([by_channel[:, 128 * g : 128 * (g + 1)] for g in range(groups)], axis=0)
    r, q = iotas((stacked.shape[0], stacked.shape[0]))
    send_ref[...] = dot(one_hot(r == by_height(q, d2n)), stacked).astype(bf16)


def second_layer_columns(hh_ref, d2n):
    cols = [jnp.concatenate([with_before(hh_ref[2 * d + kd, kh]) for d in range(d2n)], axis=0) for kd, kh in TAPS]
    return jnp.concatenate(cols, axis=1)


def delta_kernel(cot_ref, slope_ref, delta_ref):
    d2n = delta_ref.shape[0]
    count = cot_ref.shape[0]
    r, q = iotas((count, count))
    got = dot(one_hot(q == by_height(r, d2n)), cot_ref[...])
    for d in range(d2n):
        for b in range(BLOCKS):
            at = [((2 * b + i) * d2n + d) * HB for i in range(2)]
            c = jnp.concatenate([got[i : i + HB] for i in at], axis=1)
            slope = jnp.where(slope_ref[d, b * HB : (b + 1) * HB].astype(f32) > 0, 1.0, SLOPE)
            delta_ref[d, b * HB : (b + 1) * HB] = (c * slope).astype(bf16)


def diagonals(g, first, cells, cout, cin):
    lanes = 2 * cells * cin
    _, q = iotas((cout, lanes))
    w = q // cin
    ahead = jnp.zeros((cout, lanes), f32)
    behind = jnp.where(w == 2 * cells - 1, g[:cout, first + lanes : first + 2 * lanes], 0.0)
    for o in range(cells):
        x = g[o * cout : (o + 1) * cout, first : first + lanes]
        ahead = jnp.where(w // 2 == o, x, ahead)
        if o:
            behind = jnp.where(w == 2 * o - 1, x, behind)
    return ahead, behind


def width_sums(g, cells, cout, cin, place):
    lanes = 2 * cells * cin
    both = [diagonals(g, 2 * lanes * tap, cells, cout, cin) for tap in range(9)]
    ahead, behind = place([x for x, _ in both]), place([x for _, x in both])
    r, q = iotas((2 * cin, lanes))
    pick = jnp.where((q // cin % 2 == r // cin) & (q % cin == r % cin), 1.0, 0.0)
    r, q = iotas((max(cin, 8), lanes))
    every = jnp.where(q % cin == r, 1.0, 0.0)
    return [jnp.concatenate([exact_nt(pick, x), exact_nt(every, y)], axis=0) for x, y in zip(ahead, behind)]


def second_gradient_kernel(hh_ref, delta_ref, k2_ref, out_ref, t2b_ref):
    d2n = delta_ref.shape[0]
    band_back(tiled(spread_back(k2_ref[...]), W2), LZ, C2, LH, C1, puts(t2b_ref, LZ))
    delta = jnp.concatenate([delta_ref[d] for d in range(d2n)], axis=0)
    g = dot_tn(delta, second_layer_columns(hh_ref, d2n))
    none = [jnp.zeros((3 * C2, LH), f32)]
    (sums,) = width_sums(g, W2, C2, C1, lambda taps: [jnp.concatenate(taps + none, axis=0)])
    out_ref[...] = sums


def first_gradient_kernel(hh_ref, delta_ref, next_ref, t2b_ref, a_ref, two_ref, out_ref, dv_ref):
    d2n = delta_ref.shape[0]
    r, _ = iotas((ROWS, LZ))
    keep = r % HB != HB - 1
    none = jnp.zeros((HB, LZ), bf16)
    for d in range(d2n + 1):
        x = delta_ref[d] if d < d2n else next_ref[...]
        up = jnp.where(keep, pltpu.roll(x.astype(f32), ROWS - 1, 0), 0.0).astype(bf16)
        for v, y in enumerate((x, up)):
            dv_ref[d, v, :, :LZ] = y
            dv_ref[d, v, :, LZ:] = jnp.concatenate([y[HB:], none], axis=0)

    def pulled(first, kd, kh):
        v = 1 if kh == 0 else 0
        lhs = jnp.concatenate([dv_ref[d + first, v] for d in range(d2n)], axis=0)
        tap = 3 * kd + kh
        return lhs, t2b_ref[2 * LZ * tap : 2 * LZ * (tap + 1)]

    deltas, cols = [], []
    for p in range(2):
        heights = (1,) if p == 0 else (2, 0)
        for even in range(2):
            depths = ((0, 2), (1, 0)) if even else ((0, 1),)
            terms = [pulled(first, kd, kh) for first, kd in depths for kh in heights]
            back = dot(
                jnp.concatenate([lhs for lhs, _ in terms], axis=1),
                jnp.concatenate([rhs for _, rhs in terms], axis=0),
            )
            planes = [2 * d + 1 + even for d in range(d2n)]
            hidden = jnp.concatenate([hh_ref[j, 2 if p else 1] for j in planes], axis=0)
            deltas.append((back * jnp.where(hidden.astype(f32) > 0, 1.0, SLOPE)).astype(bf16))
            cols.append(
                jnp.concatenate(
                    [
                        jnp.concatenate([with_before(a_ref[2 * j + kd, INPUT_ROWS[p, kh]]) for j in planes], axis=0)
                        for kd, kh in TAPS
                    ],
                    axis=1,
                )
            )
    g = dot_tn(jnp.concatenate(deltas, axis=0), jnp.concatenate(cols, axis=0))
    before, after = [jnp.zeros((C2, LA), f32)], [jnp.zeros((128 - C2 - 3 * C1, LA), f32)]

    def place(taps):
        return [jnp.concatenate(before + taps[i : i + 3] + after, axis=0) for i in range(0, 9, 3)]

    sums = jnp.concatenate(width_sums(g, W1, C1, CIN, place), axis=0)
    out_ref[: 3 * C1] = two_ref[:, :128]
    out_ref[3 * C1 : 6 * C1] = two_ref[:, 128:256]
    out_ref[6 * C1 :] = two_ref[:, 256:] + sums


def scale_kernel(factor, sum_ref, one_ref, two_ref):
    place = (2, 0, 1)
    for tap in range(9):
        for kw in range(3):
            r, q = 3 * C1 * (tap // 4) + C1 * place[kw], C2 * (tap % 4)
            two_ref[3 * tap + kw] = sum_ref[r : r + C1, q : q + C2] * factor
            r, q = 6 * C1 + C1 * (tap // 3) + CIN * place[kw], C2 + C1 * (tap % 3)
            one_ref[3 * tap + kw] = sum_ref[r : r + CIN, q : q + C1] * factor


def gather_kernel(vol_ref, cot_ref, low_ref, out_ref, order_ref, own_ref, sems):
    planes = vol_ref.shape[1]
    d2n = planes // 4
    copies = [
        pltpu.make_async_copy(cot_ref, own_ref, sems.at[0]),
        pltpu.make_async_copy(vol_ref.at[:, planes - 3 :], low_ref, sems.at[1]),
    ]
    for copy in copies:
        copy.start()
    channels, depth, cells = cot_ref.shape
    hl = cells // 32
    order_ref[...] = channel_order()
    r, q = iotas((cells, hl * 128))
    moves = [one_hot((q // 128 == r // 32) & (q % 128 == i * 32 + r % 32)) for i in range(4)]
    copies[0].wait()
    groups = []
    for first in range(0, channels, 4):
        parts = [dot(own_ref[first + i], moves[i]) for i in range(4)]
        groups.append(((parts[0] + parts[1]) + (parts[2] + parts[3])).astype(bf16))
    x = jnp.concatenate(
        [jnp.concatenate([g[:, h * 128 : (h + 1) * 128] for g in groups], axis=1) for h in range(hl)], axis=0
    )
    x = dot_nt(x, order_ref[...]).astype(bf16)
    rows = [x[h * depth : (h + 1) * depth, 128 * g : 128 * (g + 1)] for h in range(hl) for g in range(8)]
    count = len(rows) * depth
    r, q = iotas((count, count))
    row, plane = travel_order(r, depth, d2n, hl)
    out_ref[...] = dot(one_hot(q == row * depth + plane), jnp.concatenate(rows, axis=0)).astype(bf16)
    copies[1].wait()


def scatter_kernel(d2n, got_ref, out_ref):
    channels, depth, cells = out_ref.shape
    hl = cells // 32
    count = got_ref.shape[0]
    r, q = iotas((count, count))
    row, plane = travel_order(q, depth, d2n, hl)
    got = dot(one_hot(r == row * depth + plane), got_ref[...]).astype(bf16)
    r, q = iotas((hl * 128, cells))
    moves = [one_hot((r // 128 == q // 32) & (r % 128 == i * 32 + q % 32)) for i in range(4)]
    groups = channels // 4
    for g in range(groups):
        x = jnp.concatenate(
            [got[(h * groups + g) * depth : (h * groups + g + 1) * depth] for h in range(hl)], axis=1
        )
        for i in range(4):
            out_ref[4 * g + i] = dot(x, moves[i]).astype(bf16)


def call(kernel, name, outs, *args, scratch=(), apart=()):
    return pl.pallas_call(
        kernel,
        name=name,
        in_specs=[pl.BlockSpec(memory_space=pltpu.HBM if i in apart else pltpu.VMEM) for i in range(len(args))],
        out_specs=[pl.BlockSpec(memory_space=pltpu.VMEM) for _ in outs],
        out_shape=[jax.ShapeDtypeStruct(shape, dtype) for shape, dtype in outs],
        scratch_shapes=list(scratch),
        compiler_params=pltpu.CompilerParams(vmem_limit_bytes=32 << 20),
    )(*args)


def passed_along(block, distance):
    devices = range(lax.axis_size("space"))
    return lax.ppermute(block, "space", [(i - distance, i) for i in devices if i - distance in devices])


def with_partner(block, bit):
    count = lax.axis_size("dp") * lax.axis_size("space")
    return lax.ppermute(block, ("dp", "space"), [(i, i ^ bit) for i in range(count)])


def total_and_exchange(terms, rows):
    devices = lax.axis_size("space")
    here = lax.axis_index("space")
    count = rows.shape[0] // devices
    blocks = rows.reshape(devices, count, 128)
    half = terms.shape[0] // 2
    first, second = rows.shape[0] // 2, rows.shape[0] // 2 + half
    even = here % 2 == 0
    bit = 1
    while bit < devices:
        mine = (here // bit) % 2 == 0
        pairs = blocks.reshape(devices // (2 * bit), 2, bit, count, 128)
        kept = jnp.where(mine, pairs[:, 0], pairs[:, 1])
        sent = jnp.where(mine, pairs[:, 1], pairs[:, 0]).reshape(first, 128)
        high = lax.reduce_precision(terms, 8, 7)
        rest = lax.reduce_precision(terms - high, 8, 7)
        if bit == 1:
            stay = jnp.where(even, terms[:half], terms[half:])
            high, rest = (jnp.where(even, x[half:], x[:half]) for x in (high, rest))
        else:
            stay = high + rest
        got = with_partner(jnp.concatenate([sent, high.astype(bf16), rest.astype(bf16)], axis=0), bit)
        terms = stay + (got[first:second].astype(f32) + got[second:].astype(f32))
        came = got[:first].reshape(kept.shape)
        blocks = jnp.where(mine, jnp.stack([kept, came], 1), jnp.stack([came, kept], 1))
        bit *= 2
    while bit < devices * lax.axis_size("dp"):
        terms = terms + with_partner(terms, bit)
        bit *= 2
    other = with_partner(terms, 1)
    terms = jnp.where(even, jnp.concatenate([terms, other], 0), jnp.concatenate([other, terms], 0))
    return terms, blocks.reshape(rows.shape)


def exchanged(rows):
    devices = lax.axis_size("space")
    blocks = rows.reshape(devices, rows.shape[0] // devices, 128)
    return lax.all_to_all(blocks, "space", 0, 0, tiled=True).reshape(rows.shape)


def local(volumes, kernel_one, kernel_two, cotangent):
    _, _, planes, height, width = volumes.shape
    d1n, d2n = planes // 2, planes // 4
    _, _, depth, cells = cotangent.shape
    vol, cot = volumes[0], cotangent[0]
    travelling = depth * (cells // 32) * (C2 // 4)

    low, cot_rows, order = call(
        gather_kernel,
        "gather",
        [((CIN, 3, height, width), bf16), ((travelling, 128), bf16), ((WIDE, WIDE), bf16)],
        vol,
        cot,
        scratch=[pltpu.VMEM(cot.shape, bf16), pltpu.SemaphoreType.DMA((2,))],
        apart=(0, 1),
    )
    low = passed_along(low, 1)
    cot_here = exchanged(cot_rows)

    k1 = kernel_one.transpose(2, 3, 4, 1, 0).reshape(27, CIN, C1)
    k2 = kernel_two.transpose(2, 3, 4, 1, 0).reshape(27 * C1, C2)
    a, hh, send, slope = call(
        forward_kernel,
        "forward",
        [
            ((planes + 3, 5, ROWS, LA), bf16),
            ((d1n + 1, 3, ROWS, LH), bf16),
            ((travelling, 128), bf16),
            ((d2n, ROWS, LZ), bf16),
        ],
        vol,
        low,
        k1,
        k2,
        order,
        scratch=[
            pltpu.VMEM(vol.shape, bf16),
            pltpu.VMEM((9 * 2 * LA, LH), bf16),
            pltpu.VMEM((9 * 2 * LH, LZ), bf16),
            pltpu.SemaphoreType.DMA,
        ],
        apart=(0,),
    )
    (delta,) = call(delta_kernel, "delta", [((d2n, ROWS, LZ), bf16)], cot_here, slope)
    delta_next = passed_along(delta[0], -1)
    term_two, t2b = call(
        second_gradient_kernel,
        "second_gradient",
        [((3 * C1, 384), f32), ((9 * 2 * LZ, LH), bf16)],
        hh,
        delta,
        k2,
    )
    (terms,) = call(
        first_gradient_kernel,
        "first_gradient",
        [((9 * C1, 128), f32)],
        hh,
        delta,
        delta_next,
        t2b,
        a,
        term_two,
        scratch=[pltpu.VMEM((d2n + 1, 2, ROWS, 2 * LZ), bf16)],
    )
    terms, got = total_and_exchange(terms, send)
    (out,) = call(functools.partial(scatter_kernel, d2n), "scatter", [((C2, depth, cells), bf16)], got)
    count = volumes.shape[0] * lax.axis_size("dp")
    factor = 1.0 / math.sqrt(count * depth * (height // 4) ** 2)
    one, two = call(
        functools.partial(scale_kernel, factor),
        "scale",
        [((27, CIN, C1), f32), ((27, C1, C2), f32)],
        terms,
    )
    return (
        out[None],
        one.reshape(3, 3, 3, CIN, C1).transpose(4, 3, 0, 1, 2),
        two.reshape(3, 3, 3, C1, C2).transpose(4, 3, 0, 1, 2),
    )


def solution(mesh):
    placed = (P("dp", None, "space", None, None), P(), P(), P("dp", None, None, "space"))
    return jax.shard_map(
        local,
        mesh=mesh,
        in_specs=placed,
        out_specs=(P("dp", None, None, "space"), P(), P()),
        check_vma=False,
    )
```

```python
import functools
import math

import jax
import jax.numpy as jnp
from jax import lax
from jax.experimental import pallas as pl
from jax.experimental.pallas import tpu as pltpu
from jax.sharding import PartitionSpec as P

f32 = jnp.float32
bf16 = jnp.bfloat16

SLOPE = 0.3
BLOCKS = 4
HB = 32
CIN, C1, C2 = 4, 16, 32
W0, W1, W2 = 32, 16, 8
ROWS = BLOCKS * HB
LA, LH, LZ = W0 * CIN, W1 * C1, W2 * C2
WIDE = BLOCKS * LZ
TAPS = [(kd, kh) for kd in range(3) for kh in range(3)]
INPUT_ROWS = {(0, 0): 4, (0, 1): 0, (0, 2): 1, (1, 0): 1, (1, 1): 2, (1, 2): 3}


def dot(a, b):
    return jnp.dot(a, b, preferred_element_type=f32)


def dot_nt(a, b):
    return lax.dot_general(a, b, (((1,), (1,)), ((), ())), preferred_element_type=f32)


def dot_tn(a, b):
    return lax.dot_general(a, b, (((0,), (0,)), ((), ())), preferred_element_type=f32)


def exact_nt(a, b):
    return lax.dot_general(
        a, b, (((1,), (1,)), ((), ())), precision=lax.Precision.HIGHEST, preferred_element_type=f32
    )


def iotas(shape):
    rows, lanes = shape
    return lax.broadcasted_iota(jnp.int32, (rows, 1), 0), lax.broadcasted_iota(jnp.int32, (1, lanes), 1)


def one_hot(mask):
    return jnp.where(mask, 1.0, 0.0).astype(bf16)


def width_order():
    r, q = iotas((CIN * 128, CIN * 128))
    return one_hot(r == (q % CIN) * 128 + (q // LA) * W0 + (q // CIN) % W0)


def height_order():
    r, q = iotas((5 * HB, 4 * HB))
    return one_hot(q == 4 * (r % HB) + jnp.where(r // HB == 4, -1, r // HB))


def channel_order():
    r, q = iotas((WIDE, WIDE))
    cells = BLOCKS * W2
    return one_hot(r == (q % cells) * C2 + q // cells)


def arrange_planes(planes, count, put):
    x = jnp.concatenate([planes(c) for c in range(CIN)], axis=1)
    y = dot(x, width_order()).astype(bf16)
    order = height_order()
    for d in range(count):
        z = dot(order, y[d * 128 : (d + 1) * 128]).astype(bf16)
        for v in range(5):
            put(d, v, [z[v * HB : (v + 1) * HB, b * LA : (b + 1) * LA] for b in range(BLOCKS)])


def with_before(x):
    return jnp.concatenate([x, jnp.concatenate([jnp.zeros_like(x[:HB]), x[:-HB]], axis=0)], axis=1)


def band(taps, rows, cin, cols, cout, put):
    r, q = iotas((rows, cols))
    w, o = r // cin, q // cout
    rel = w - 2 * o + 1
    last = (w == rows // cin - 1) & (o == 0)
    for tap in range(9):
        e = [taps(3 * tap + kw) for kw in range(3)]
        own = jnp.where(rel == 0, e[0], jnp.where(rel == 1, e[1], jnp.where(rel == 2, e[2], 0.0)))
        put(tap, own.astype(bf16), jnp.where(last, e[0], 0.0).astype(bf16))


def band_back(taps, rows, cout, cols, cin, put):
    r, q = iotas((rows, cols))
    w, o = q // cin, r // cout
    rel = w - 2 * o + 1
    last = (w == cols // cin - 1) & (o == 0)
    for tap in range(9):
        e = [taps(3 * tap + kw) for kw in range(3)]
        own = jnp.where(rel == 0, e[0], jnp.where(rel == 1, e[1], jnp.where(rel == 2, e[2], 0.0)))
        put(tap, own.astype(bf16), jnp.where(last, e[0], 0.0).astype(bf16))


def spread(k, cols):
    c, q = iotas((k.shape[1], cols))
    return dot(k, one_hot(q % k.shape[1] == c))


def spread_back(k2):
    r, q = iotas((C2, C2))
    flipped = dot_nt(one_hot(r == q), k2).astype(bf16)
    flipped = jnp.concatenate([flipped, jnp.zeros((C2, 512 - 27 * C1), bf16)], axis=1)
    stacked = jnp.concatenate([flipped[:, 128 * i : 128 * (i + 1)] for i in range(4)], axis=0)
    r, q = iotas((128, LH))
    parts = [dot(stacked, one_hot((r // C1 == g) & (q % C1 == r % C1))) for g in range(8)]
    return lambda t: parts[t % 8][C2 * (t // 8) : C2 * (t // 8 + 1)]


def shifted_down(x, keep):
    return jnp.where(keep, pltpu.roll(x.astype(f32), 1, 0), 0.0).astype(bf16)


def travel_order(r, depth, d2n, hl):
    groups = hl * C2 // 4
    return (r // d2n) % groups, r // (groups * d2n) * d2n + r % d2n


def by_height(r, d2n):
    group, plane, h2 = r // (d2n * HB), (r // HB) % d2n, r % HB
    return (h2 * (C2 // 4) + group) * d2n + plane


def puts(ref, half):
    def put(tap, own, other):
        ref[2 * half * tap : 2 * half * tap + half] = own
        ref[2 * half * tap + half : 2 * half * (tap + 1)] = other

    return put


def tiled(each, times):
    return lambda t: jnp.concatenate([each(t)] * times, axis=0)


def forward_kernel(
    vol_ref, low_ref, k1_ref, k2_ref, a_hbm, hh_ref, send_ref, slope_ref, a_ref, t1_ref, t2_ref, sem
):
    count = vol_ref.shape[1]
    planes = hh_ref.shape[0]
    d2n = slope_ref.shape[0]
    copy = pltpu.make_async_copy(a_ref, a_hbm, sem)

    def put_from(first):
        def put(d, v, blocks):
            for b, x in enumerate(blocks):
                a_ref[first + d, v, b * HB : (b + 1) * HB] = x

        return put

    k1 = jnp.concatenate([k1_ref[t].astype(f32) for t in range(27) for _ in range(16 // CIN)], axis=0)
    k1 = spread(k1.astype(bf16), LH)
    band(tiled(lambda t: k1[16 * t : 16 * (t + 1)], LA // 16), LA, CIN, LH, C1, puts(t1_ref, LA))
    k2 = spread(k2_ref[...], LZ)
    band(tiled(lambda t: k2[C1 * t : C1 * (t + 1)], W1), LH, C1, LZ, C2, puts(t2_ref, LH))
    arrange_planes(lambda c: low_ref[c].reshape(3 * 128, 128), 3, put_from(0))
    arrange_planes(lambda c: vol_ref[c].reshape(count * 128, 128), count, put_from(3))
    copy.start()

    r, _ = iotas((planes * ROWS, LH))
    keep = r % HB != 0
    for p in range(2):
        cols = [
            jnp.concatenate([with_before(a_ref[2 * j + kd, INPUT_ROWS[p, kh]]) for j in range(planes)], axis=0)
            for kd, kh in TAPS
        ]
        linear = dot(jnp.concatenate(cols, axis=1), t1_ref[...])
        hidden = jnp.where(linear > 0, linear, SLOPE * linear).astype(bf16)
        variants = [(1, hidden)] if p == 0 else [(2, hidden), (0, shifted_down(hidden, keep))]
        for v, x in variants:
            for j in range(planes):
                hh_ref[j, v] = x[j * ROWS : (j + 1) * ROWS]

    linear = dot(second_layer_columns(hh_ref, d2n), t2_ref[...])
    out = jnp.where(linear > 0, linear, SLOPE * linear).astype(bf16)
    positive = jnp.where(linear > 0, 1.0, 0.0).astype(bf16)
    for d in range(d2n):
        slope_ref[d] = positive[d * ROWS : (d + 1) * ROWS]
    wide = jnp.concatenate(
        [
            jnp.concatenate([out[d * ROWS + b * HB : d * ROWS + (b + 1) * HB] for b in range(BLOCKS)], axis=1)
            for d in range(d2n)
        ],
        axis=0,
    )
    groups = C2 // 4
    by_channel = dot(wide, channel_order()).astype(bf16)
    stacked = jnp.concatenate([by_channel[:, 128 * g : 128 * (g + 1)] for g in range(groups)], axis=0)
    r, q = iotas((stacked.shape[0], stacked.shape[0]))
    send_ref[...] = dot(one_hot(r == by_height(q, d2n)), stacked).astype(bf16)
    copy.wait()


def second_layer_columns(hh_ref, d2n):
    cols = [jnp.concatenate([with_before(hh_ref[2 * d + kd, kh]) for d in range(d2n)], axis=0) for kd, kh in TAPS]
    return jnp.concatenate(cols, axis=1)


def delta_kernel(cot_ref, slope_ref, delta_ref):
    d2n = delta_ref.shape[0]
    devices, lines, _ = cot_ref.shape
    hl = lines // d2n
    r, q = iotas((d2n * HB, devices * lines))
    plane, h2 = r // HB, r % HB
    order = one_hot(q == h2 // hl * lines + h2 % hl * d2n + plane)
    got = dot(order, jnp.concatenate([cot_ref[i] for i in range(devices)], axis=0))
    for d in range(d2n):
        for b in range(BLOCKS):
            c = got[d * HB : (d + 1) * HB, b * LZ : (b + 1) * LZ]
            slope = jnp.where(slope_ref[d, b * HB : (b + 1) * HB].astype(f32) > 0, 1.0, SLOPE)
            delta_ref[d, b * HB : (b + 1) * HB] = (c * slope).astype(bf16)


def diagonals(g, first, cells, cout, cin):
    lanes = 2 * cells * cin
    _, q = iotas((cout, lanes))
    w = q // cin
    ahead = jnp.zeros((cout, lanes), f32)
    behind = jnp.where(w == 2 * cells - 1, g[:cout, first + lanes : first + 2 * lanes], 0.0)
    for o in range(cells):
        x = g[o * cout : (o + 1) * cout, first : first + lanes]
        ahead = jnp.where(w // 2 == o, x, ahead)
        if o:
            behind = jnp.where(w == 2 * o - 1, x, behind)
    return ahead, behind


def width_sums(g, cells, cout, cin, place):
    lanes = 2 * cells * cin
    both = [diagonals(g, 2 * lanes * tap, cells, cout, cin) for tap in range(9)]
    ahead, behind = place([x for x, _ in both]), place([x for _, x in both])
    r, q = iotas((2 * cin, lanes))
    pick = jnp.where((q // cin % 2 == r // cin) & (q % cin == r % cin), 1.0, 0.0)
    r, q = iotas((max(cin, 8), lanes))
    every = jnp.where(q % cin == r, 1.0, 0.0)
    return [jnp.concatenate([exact_nt(pick, x), exact_nt(every, y)], axis=0) for x, y in zip(ahead, behind)]


def second_gradient_kernel(hh_ref, delta_ref, k2_ref, a_hbm, out_ref, t2b_ref, a_ref, sem):
    copy = pltpu.make_async_copy(a_hbm, a_ref, sem)
    copy.start()
    d2n = delta_ref.shape[0]
    delta = jnp.concatenate([delta_ref[d] for d in range(d2n)], axis=0)
    g = dot_tn(delta, second_layer_columns(hh_ref, d2n))
    none = [jnp.zeros((3 * C2, LH), f32)]
    (sums,) = width_sums(g, W2, C2, C1, lambda taps: [jnp.concatenate(taps + none, axis=0)])
    out_ref[...] = sums
    band_back(tiled(spread_back(k2_ref[...]), W2), LZ, C2, LH, C1, puts(t2b_ref, LZ))
    copy.wait()


def first_gradient_kernel(hh_ref, delta_ref, next_ref, t2b_ref, a_ref, two_ref, out_ref, dv_ref):
    d2n = delta_ref.shape[0]
    r, _ = iotas((ROWS, LZ))
    keep = r % HB != HB - 1
    none = jnp.zeros((HB, LZ), bf16)
    for d in range(d2n + 1):
        x = delta_ref[d] if d < d2n else next_ref[...]
        up = jnp.where(keep, pltpu.roll(x.astype(f32), ROWS - 1, 0), 0.0).astype(bf16)
        for v, y in enumerate((x, up)):
            dv_ref[d, v, :, :LZ] = y
            dv_ref[d, v, :, LZ:] = jnp.concatenate([y[HB:], none], axis=0)

    def pulled(first, kd, kh):
        v = 1 if kh == 0 else 0
        lhs = jnp.concatenate([dv_ref[d + first, v] for d in range(d2n)], axis=0)
        tap = 3 * kd + kh
        return lhs, t2b_ref[2 * LZ * tap : 2 * LZ * (tap + 1)]

    deltas, planes = [], []
    for p in range(2):
        heights = (1,) if p == 0 else (2, 0)
        for even in range(2):
            depths = ((0, 2), (1, 0)) if even else ((0, 1),)
            terms = [pulled(first, kd, kh) for first, kd in depths for kh in heights]
            back = dot(
                jnp.concatenate([lhs for lhs, _ in terms], axis=1),
                jnp.concatenate([rhs for _, rhs in terms], axis=0),
            )
            here = [(p, 2 * d + 1 + even) for d in range(d2n)]
            hidden = jnp.concatenate([hh_ref[j, 2 if p else 1] for _, j in here], axis=0)
            deltas.append((back * jnp.where(hidden.astype(f32) > 0, 1.0, SLOPE)).astype(bf16))
            planes += here
    cols = [
        jnp.concatenate([with_before(a_ref[2 * j + kd, INPUT_ROWS[p, kh]]) for p, j in planes], axis=0)
        for kd, kh in TAPS
    ]
    g = dot_tn(jnp.concatenate(deltas, axis=0), jnp.concatenate(cols, axis=1))
    before, after = [jnp.zeros((C2, LA), f32)], [jnp.zeros((128 - C2 - 3 * C1, LA), f32)]

    def place(taps):
        return [jnp.concatenate(before + taps[i : i + 3] + after, axis=0) for i in range(0, 9, 3)]

    sums = jnp.concatenate(width_sums(g, W1, C1, CIN, place), axis=0)
    out_ref[: 3 * C1] = two_ref[:, :128]
    out_ref[3 * C1 : 6 * C1] = two_ref[:, 128:256]
    out_ref[6 * C1 :] = two_ref[:, 256:] + sums


def scale_kernel(factor, sum_ref, one_ref, two_ref):
    place = (2, 0, 1)
    for tap in range(9):
        for kw in range(3):
            r, q = 3 * C1 * (tap // 4) + C1 * place[kw], C2 * (tap % 4)
            two_ref[3 * tap + kw] = sum_ref[r : r + C1, q : q + C2] * factor
            r, q = 6 * C1 + C1 * (tap // 3) + CIN * place[kw], C2 + C1 * (tap % 3)
            one_ref[3 * tap + kw] = sum_ref[r : r + CIN, q : q + C1] * factor


def gather_kernel(
    vol_hbm, cot_hbm, k1_hbm, k2_hbm, vol_ref, out_ref, k1_ref, k2_ref, cot_ref, order_ref, sems
):
    d2n = vol_ref.shape[1] // 4
    copies = [
        pltpu.make_async_copy(x, y, sems.at[i])
        for i, (x, y) in enumerate(
            [(cot_hbm, cot_ref), (vol_hbm, vol_ref), (k1_hbm, k1_ref), (k2_hbm, k2_ref)]
        )
    ]
    for copy in copies:
        copy.start()
    channels, depth, cells = cot_ref.shape
    hl = cells // 32
    r, q = iotas((WIDE, WIDE))
    order_ref[...] = one_hot(q == (r % (BLOCKS * W2)) * C2 + r // (BLOCKS * W2))
    r, q = iotas((cells, hl * 128))
    moves = [one_hot((q // 128 == r // 32) & (q % 128 == i * 32 + r % 32)) for i in range(4)]
    copies[0].wait()
    parts = [
        dot(jnp.concatenate([cot_ref[first + i] for first in range(0, channels, 4)], axis=0), moves[i])
        for i in range(4)
    ]
    together = ((parts[0] + parts[1]) + (parts[2] + parts[3])).astype(bf16)
    groups = [together[i * depth : (i + 1) * depth] for i in range(channels // 4)]
    x = jnp.concatenate(
        [jnp.concatenate([g[:, h * 128 : (h + 1) * 128] for g in groups], axis=1) for h in range(hl)], axis=0
    )
    x = dot(x, order_ref[...]).astype(bf16)
    for device in range(out_ref.shape[0]):
        for h in range(hl):
            at = h * depth + device * d2n
            out_ref[device, h * d2n : (h + 1) * d2n] = x[at : at + d2n]
    for copy in copies[1:]:
        copy.wait()


def last_planes_kernel(vol_ref, low_ref):
    low_ref[...] = vol_ref[:, vol_ref.shape[1] - 3 :]


def scatter_kernel(d2n, got_ref, out_ref):
    channels, depth, cells = out_ref.shape
    hl = cells // 32
    count = got_ref.shape[0]
    r, q = iotas((count, count))
    row, plane = travel_order(q, depth, d2n, hl)
    got = dot(one_hot(r == row * depth + plane), got_ref[...]).astype(bf16)
    r, q = iotas((hl * 128, cells))
    moves = [one_hot((r // 128 == q // 32) & (r % 128 == i * 32 + q % 32)) for i in range(4)]
    groups = channels // 4
    for g in range(groups):
        x = jnp.concatenate(
            [got[(h * groups + g) * depth : (h * groups + g + 1) * depth] for h in range(hl)], axis=1
        )
        for i in range(4):
            out_ref[4 * g + i] = dot(x, moves[i]).astype(bf16)


def call(kernel, name, outs, *args, scratch=(), apart=(), apart_out=()):
    return pl.pallas_call(
        kernel,
        name=name,
        in_specs=[pl.BlockSpec(memory_space=pltpu.HBM if i in apart else pltpu.VMEM) for i in range(len(args))],
        out_specs=[
            pl.BlockSpec(memory_space=pltpu.HBM if i in apart_out else pltpu.VMEM) for i in range(len(outs))
        ],
        out_shape=[
            pltpu.HBM(shape, dtype) if i in apart_out else jax.ShapeDtypeStruct(shape, dtype)
            for i, (shape, dtype) in enumerate(outs)
        ],
        scratch_shapes=list(scratch),
        compiler_params=pltpu.CompilerParams(vmem_limit_bytes=32 << 20),
    )(*[pltpu.with_memory_space_constraint(x, pltpu.HBM) if i in apart else x for i, x in enumerate(args)])


def passed_along(block, distance):
    devices = range(lax.axis_size("space"))
    return lax.ppermute(block, "space", [(i - distance, i) for i in devices if i - distance in devices])


def with_partner(block, bit):
    count = lax.axis_size("dp") * lax.axis_size("space")
    return lax.ppermute(block, ("dp", "space"), [(i, i ^ bit) for i in range(count)])


def total_and_exchange(terms, rows):
    devices = lax.axis_size("space")
    here = lax.axis_index("space")
    count = rows.shape[0] // devices
    blocks = rows.reshape(devices, count, 128)
    half = terms.shape[0] // 2
    first, second = rows.shape[0] // 2, rows.shape[0] // 2 + half
    even = here % 2 == 0
    bit = 1
    while bit < devices:
        mine = (here // bit) % 2 == 0
        pairs = blocks.reshape(devices // (2 * bit), 2, bit, count, 128)
        kept = jnp.where(mine, pairs[:, 0], pairs[:, 1])
        sent = jnp.where(mine, pairs[:, 1], pairs[:, 0]).reshape(first, 128)
        high = lax.reduce_precision(terms, 8, 7)
        rest = lax.reduce_precision(terms - high, 8, 7)
        if bit == 1:
            stay = jnp.where(even, terms[:half], terms[half:])
            high, rest = (jnp.where(even, x[half:], x[:half]) for x in (high, rest))
        else:
            stay = high + rest
        got = with_partner(jnp.concatenate([sent, high.astype(bf16), rest.astype(bf16)], axis=0), bit)
        terms = stay + (got[first:second].astype(f32) + got[second:].astype(f32))
        came = got[:first].reshape(kept.shape)
        blocks = jnp.where(mine, jnp.stack([kept, came], 1), jnp.stack([came, kept], 1))
        bit *= 2
    while bit < devices * lax.axis_size("dp"):
        terms = terms + with_partner(terms, bit)
        bit *= 2
    return terms, blocks.reshape(rows.shape)


def rejoined(half):
    other = with_partner(half, 1)
    even = lax.axis_index("space") % 2 == 0
    return jnp.where(even, jnp.concatenate([half, other], 0), jnp.concatenate([other, half], 0))


def local(volumes, kernel_one, kernel_two, cotangent):
    _, _, planes, height, width = volumes.shape
    d1n, d2n = planes // 2, planes // 4
    _, _, depth, cells = cotangent.shape
    vol, cot = volumes[0], cotangent[0]
    devices = lax.axis_size("space")
    travelling = depth * (cells // 32) * (C2 // 4)

    k1 = kernel_one.transpose(2, 3, 4, 1, 0).reshape(27, CIN, C1)
    k2 = kernel_two.transpose(2, 3, 4, 1, 0).reshape(27 * C1, C2)
    vol, cot_rows, k1, k2 = call(
        gather_kernel,
        "gather",
        [(vol.shape, bf16), ((devices, depth // devices * (cells // 32), WIDE), bf16), (k1.shape, bf16), (k2.shape, bf16)],
        vol,
        cot,
        k1,
        k2,
        scratch=[
            pltpu.VMEM(cot.shape, bf16),
            pltpu.VMEM((WIDE, WIDE), bf16),
            pltpu.SemaphoreType.DMA((4,)),
        ],
        apart=(0, 1, 2, 3),
    )
    (low,) = call(last_planes_kernel, "last_planes", [((CIN, 3, height, width), bf16)], vol)
    low = passed_along(low, 1)
    cot_here = lax.all_to_all(cot_rows, "space", 0, 0, tiled=True)

    a, hh, send, slope = call(
        forward_kernel,
        "forward",
        [
            ((planes + 3, 5, ROWS, LA), bf16),
            ((d1n + 1, 3, ROWS, LH), bf16),
            ((travelling, 128), bf16),
            ((d2n, ROWS, LZ), bf16),
        ],
        vol,
        low,
        k1,
        k2,
        scratch=[
            pltpu.VMEM((planes + 3, 5, ROWS, LA), bf16),
            pltpu.VMEM((9 * 2 * LA, LH), bf16),
            pltpu.VMEM((9 * 2 * LH, LZ), bf16),
            pltpu.SemaphoreType.DMA,
        ],
        apart_out=(0,),
    )
    (delta,) = call(delta_kernel, "delta", [((d2n, ROWS, LZ), bf16)], cot_here, slope)
    delta_next = passed_along(delta[0], -1)
    term_two, t2b, a = call(
        second_gradient_kernel,
        "second_gradient",
        [((3 * C1, 384), f32), ((9 * 2 * LZ, LH), bf16), (a.shape, bf16)],
        hh,
        delta,
        k2,
        a,
        scratch=[pltpu.SemaphoreType.DMA],
        apart=(3,),
    )
    (terms,) = call(
        first_gradient_kernel,
        "first_gradient",
        [((9 * C1, 128), f32)],
        hh,
        delta,
        delta_next,
        t2b,
        a,
        term_two,
        scratch=[pltpu.VMEM((d2n + 1, 2, ROWS, 2 * LZ), bf16)],
    )
    half, got = total_and_exchange(terms, send)
    (out,) = call(functools.partial(scatter_kernel, d2n), "scatter", [((C2, depth, cells), bf16)], got)
    half, out = lax.optimization_barrier((half, out))
    terms = rejoined(half)
    count = volumes.shape[0] * lax.axis_size("dp")
    factor = 1.0 / math.sqrt(count * depth * (height // 4) ** 2)
    one, two = call(
        functools.partial(scale_kernel, factor),
        "scale",
        [((27, CIN, C1), f32), ((27, C1, C2), f32)],
        terms,
    )
    return (
        out[None],
        one.reshape(3, 3, 3, CIN, C1).transpose(4, 3, 0, 1, 2),
        two.reshape(3, 3, 3, C1, C2).transpose(4, 3, 0, 1, 2),
    )


def solution(mesh):
    placed = (P("dp", None, "space", None, None), P(), P(), P("dp", None, None, "space"))
    return jax.shard_map(
        local,
        mesh=mesh,
        in_specs=placed,
        out_specs=(P("dp", None, None, "space"), P(), P()),
        check_vma=False,
    )
```

```python
import functools
import math

import jax
import jax.numpy as jnp
from jax import lax
from jax.experimental import pallas as pl
from jax.experimental.pallas import tpu as pltpu
from jax.sharding import PartitionSpec as P

f32 = jnp.float32
bf16 = jnp.bfloat16

SLOPE = 0.3
BLOCKS = 4
HB = 32
CIN, C1, C2 = 4, 16, 32
W0, W1, W2 = 32, 16, 8
ROWS = BLOCKS * HB
LA, LH, LZ = W0 * CIN, W1 * C1, W2 * C2
EDGE = LA // BLOCKS
WIDE = BLOCKS * LZ
TAPS = [(kd, kh) for kd in range(3) for kh in range(3)]
INPUT_ROWS = {(0, 0): 4, (0, 1): 0, (0, 2): 1, (1, 0): 1, (1, 1): 2, (1, 2): 3}


def dot(a, b):
    return jnp.dot(a, b, preferred_element_type=f32)


def dot_nt(a, b):
    return lax.dot_general(a, b, (((1,), (1,)), ((), ())), preferred_element_type=f32)


def dot_tn(a, b):
    return lax.dot_general(a, b, (((0,), (0,)), ((), ())), preferred_element_type=f32)


def exact_nt(a, b):
    return lax.dot_general(
        a, b, (((1,), (1,)), ((), ())), precision=lax.Precision.HIGHEST, preferred_element_type=f32
    )


def iotas(shape):
    rows, lanes = shape
    return lax.broadcasted_iota(jnp.int32, (rows, 1), 0), lax.broadcasted_iota(jnp.int32, (1, lanes), 1)


def one_hot(mask):
    return jnp.where(mask, 1.0, 0.0).astype(bf16)


def width_order():
    r, q = iotas((CIN * 128, (CIN + 1) * 128))
    own = (q % CIN) * 128 + (q // LA) * W0 + (q // CIN) % W0
    edge = (q % CIN) * 128 + (q % LA) // EDGE * W0 - 1
    return one_hot(r == jnp.where(q < CIN * 128, own, jnp.where(q % LA < EDGE, -1, edge)))


def height_order():
    r, q = iotas((5 * HB, 4 * HB))
    return one_hot(q == 4 * (r % HB) + jnp.where(r // HB == 4, -1, r // HB))


def channel_order():
    r, q = iotas((WIDE, WIDE))
    cells = BLOCKS * W2
    return one_hot(r == (q % cells) * C2 + q // cells)


def arrange_planes(planes, count, put):
    x = jnp.concatenate([planes(c) for c in range(CIN)], axis=1)
    y = dot(x, width_order()).astype(bf16)
    order = height_order()
    for d in range(count):
        z = dot(order, y[d * 128 : (d + 1) * 128]).astype(bf16)
        for v in range(5):
            put(d, v, [z[v * HB : (v + 1) * HB, b * LA : (b + 1) * LA] for b in range(BLOCKS + 1)])


def with_before(x):
    return jnp.concatenate([x, jnp.concatenate([jnp.zeros_like(x[:HB]), x[:-HB]], axis=0)], axis=1)


def first_layer_columns(a_ref, planes):
    _, q = iotas((HB, LA))
    times = [one_hot(q // CIN % 8 == t) for t in range(8)]
    blocks = [one_hot(q // EDGE == b) for b in range(BLOCKS)]
    cols = [[] for _ in range(11)]
    for p, j in planes:
        x = [a_ref[2 * j + kd, INPUT_ROWS[p, kh]] for kd, kh in TAPS]
        edges = [y[ROWS:] for y in x]
        eight = edges[0] * times[0]
        for t in range(1, 8):
            eight = eight + edges[t] * times[t]
        x = [y[:ROWS] for y in x]
        for y in (eight, edges[8] * times[0]):
            x.append(jnp.concatenate([y * m for m in blocks], axis=0))
        for col, y in zip(cols, x):
            col.append(y)
    return jnp.concatenate([jnp.concatenate(col, axis=0) for col in cols], axis=1)


def band(taps, rows, cin, cols, cout, put):
    r, q = iotas((rows, cols))
    w, o = r // cin, q // cout
    rel = w - 2 * o + 1
    last = (w == rows // cin - 1) & (o == 0)
    for tap in range(9):
        e = [taps(3 * tap + kw) for kw in range(3)]
        own = jnp.where(rel == 0, e[0], jnp.where(rel == 1, e[1], jnp.where(rel == 2, e[2], 0.0)))
        put(tap, own.astype(bf16), jnp.where(last, e[0], 0.0).astype(bf16))


def band_back(taps, rows, cout, cols, cin, put):
    r, q = iotas((rows, cols))
    w, o = q // cin, r // cout
    rel = w - 2 * o + 1
    last = (w == cols // cin - 1) & (o == 0)
    for tap in range(9):
        e = [taps(3 * tap + kw) for kw in range(3)]
        own = jnp.where(rel == 0, e[0], jnp.where(rel == 1, e[1], jnp.where(rel == 2, e[2], 0.0)))
        put(tap, own.astype(bf16), jnp.where(last, e[0], 0.0).astype(bf16))


def spread(k, cols):
    c, q = iotas((k.shape[1], cols))
    return dot(k, one_hot(q % k.shape[1] == c))


def spread_back(k2):
    r, q = iotas((C2, C2))
    flipped = dot_nt(one_hot(r == q), k2).astype(bf16)
    flipped = jnp.concatenate([flipped, jnp.zeros((C2, 512 - 27 * C1), bf16)], axis=1)
    stacked = jnp.concatenate([flipped[:, 128 * i : 128 * (i + 1)] for i in range(4)], axis=0)
    r, q = iotas((128, LH))
    parts = [dot(stacked, one_hot((r // C1 == g) & (q % C1 == r % C1))) for g in range(8)]
    return lambda t: parts[t % 8][C2 * (t // 8) : C2 * (t // 8 + 1)]


def shifted_down(x, keep):
    return jnp.where(keep, pltpu.roll(x.astype(f32), 1, 0), 0.0).astype(bf16)


def travel_order(r, depth, d2n, hl):
    groups = hl * C2 // 4
    return (r // d2n) % groups, r // (groups * d2n) * d2n + r % d2n


def by_height(r, d2n):
    group, plane, h2 = r // (d2n * HB), (r // HB) % d2n, r % HB
    return (h2 * (C2 // 4) + group) * d2n + plane


def puts(ref, half):
    def put(tap, own, other):
        ref[2 * half * tap : 2 * half * tap + half] = own
        ref[2 * half * tap + half : 2 * half * (tap + 1)] = other

    return put


def tiled(each, times):
    return lambda t: jnp.concatenate([each(t)] * times, axis=0)


def forward_kernel(
    vol_ref, low_ref, k1_ref, k2_ref, a_hbm, hh_ref, send_ref, slope_ref, a_ref, t1_ref, t2_ref, sem
):
    count = vol_ref.shape[1]
    planes = hh_ref.shape[0]
    d2n = slope_ref.shape[0]
    copy = pltpu.make_async_copy(a_ref, a_hbm, sem)

    def put_from(first):
        def put(d, v, blocks):
            for b, x in enumerate(blocks):
                a_ref[first + d, v, b * HB : (b + 1) * HB] = x

        return put

    k1 = jnp.concatenate([k1_ref[t].astype(f32) for t in range(27) for _ in range(16 // CIN)], axis=0)
    k1 = spread(k1.astype(bf16), LH)
    def put_own(tap, own, _):
        t1_ref[LA * tap : LA * (tap + 1)] = own

    band(tiled(lambda t: k1[16 * t : 16 * (t + 1)], LA // 16), LA, CIN, LH, C1, put_own)
    _, q = iotas((LA, LH))
    for i, taps in enumerate((range(8), [8] * 8)):
        edge = jnp.concatenate([k1[48 * t : 48 * t + CIN] for _ in range(BLOCKS) for t in taps], axis=0)
        t1_ref[LA * (9 + i) : LA * (10 + i)] = jnp.where(q < C1, edge, 0.0).astype(bf16)
    k2 = spread(k2_ref[...], LZ)
    band(tiled(lambda t: k2[C1 * t : C1 * (t + 1)], W1), LH, C1, LZ, C2, puts(t2_ref, LH))
    arrange_planes(lambda c: low_ref[c].reshape(3 * 128, 128), 3, put_from(0))
    arrange_planes(lambda c: vol_ref[c].reshape(count * 128, 128), count, put_from(3))
    copy.start()

    r, _ = iotas((planes * ROWS, LH))
    keep = r % HB != 0
    for p in range(2):
        linear = dot(first_layer_columns(a_ref, [(p, j) for j in range(planes)]), t1_ref[...])
        hidden = jnp.where(linear > 0, linear, SLOPE * linear).astype(bf16)
        variants = [(1, hidden)] if p == 0 else [(2, hidden), (0, shifted_down(hidden, keep))]
        for v, x in variants:
            for j in range(planes):
                hh_ref[j, v] = x[j * ROWS : (j + 1) * ROWS]

    linear = dot(second_layer_columns(hh_ref, d2n), t2_ref[...])
    out = jnp.where(linear > 0, linear, SLOPE * linear).astype(bf16)
    positive = jnp.where(linear > 0, 1.0, 0.0).astype(bf16)
    for d in range(d2n):
        slope_ref[d] = positive[d * ROWS : (d + 1) * ROWS]
    wide = jnp.concatenate(
        [
            jnp.concatenate([out[d * ROWS + b * HB : d * ROWS + (b + 1) * HB] for b in range(BLOCKS)], axis=1)
            for d in range(d2n)
        ],
        axis=0,
    )
    groups = C2 // 4
    by_channel = dot(wide, channel_order()).astype(bf16)
    stacked = jnp.concatenate([by_channel[:, 128 * g : 128 * (g + 1)] for g in range(groups)], axis=0)
    r, q = iotas((stacked.shape[0], stacked.shape[0]))
    send_ref[...] = dot(one_hot(r == by_height(q, d2n)), stacked).astype(bf16)
    copy.wait()


def second_layer_columns(hh_ref, d2n):
    cols = [jnp.concatenate([with_before(hh_ref[2 * d + kd, kh]) for d in range(d2n)], axis=0) for kd, kh in TAPS]
    return jnp.concatenate(cols, axis=1)


def delta_kernel(cot_ref, slope_ref, delta_ref):
    d2n = delta_ref.shape[0]
    devices, lines, _ = cot_ref.shape
    hl = lines // d2n
    r, q = iotas((d2n * HB, devices * lines))
    plane, h2 = r // HB, r % HB
    order = one_hot(q == h2 // hl * lines + h2 % hl * d2n + plane)
    got = dot(order, jnp.concatenate([cot_ref[i] for i in range(devices)], axis=0))
    for d in range(d2n):
        for b in range(BLOCKS):
            c = got[d * HB : (d + 1) * HB, b * LZ : (b + 1) * LZ]
            slope = jnp.where(slope_ref[d, b * HB : (b + 1) * HB].astype(f32) > 0, 1.0, SLOPE)
            delta_ref[d, b * HB : (b + 1) * HB] = (c * slope).astype(bf16)


def diagonals(x, before, cells, cout, cin):
    lanes = 2 * cells * cin
    _, q = iotas((cout, lanes))
    w = q // cin
    ahead = jnp.zeros((cout, lanes), f32)
    behind = jnp.zeros((cout, lanes), f32)
    for o in range(cells):
        y = x[o * cout : (o + 1) * cout]
        ahead = jnp.where(w // 2 == o, y, ahead)
        if o:
            behind = jnp.where(w == 2 * o - 1, y, behind)
    return ahead, behind + before


def width_sums(own, before, cells, cout, cin, place):
    lanes = 2 * cells * cin
    both = [diagonals(own(tap), before(tap), cells, cout, cin) for tap in range(9)]
    ahead, behind = place([x for x, _ in both]), place([x for _, x in both])
    r, q = iotas((2 * cin, lanes))
    pick = jnp.where((q // cin % 2 == r // cin) & (q % cin == r % cin), 1.0, 0.0)
    r, q = iotas((max(cin, 8), lanes))
    every = jnp.where(q % cin == r, 1.0, 0.0)
    return [jnp.concatenate([exact_nt(pick, x), exact_nt(every, y)], axis=0) for x, y in zip(ahead, behind)]


def second_gradient_kernel(hh_ref, delta_ref, k2_ref, a_hbm, out_ref, t2b_ref, a_ref, sem):
    copy = pltpu.make_async_copy(a_hbm, a_ref, sem)
    copy.start()
    d2n = delta_ref.shape[0]
    delta = jnp.concatenate([delta_ref[d] for d in range(d2n)], axis=0)
    g = dot_tn(delta, second_layer_columns(hh_ref, d2n))
    none = [jnp.zeros((3 * C2, LH), f32)]
    _, q = iotas((C2, LH))
    (sums,) = width_sums(
        lambda tap: g[:, 2 * LH * tap : 2 * LH * tap + LH],
        lambda tap: jnp.where(q // C1 == W1 - 1, g[:C2, 2 * LH * tap + LH : 2 * LH * (tap + 1)], 0.0),
        W2,
        C2,
        C1,
        lambda taps: [jnp.concatenate(taps + none, axis=0)],
    )
    out_ref[...] = sums
    band_back(tiled(spread_back(k2_ref[...]), W2), LZ, C2, LH, C1, puts(t2b_ref, LZ))
    copy.wait()


def first_gradient_kernel(hh_ref, delta_ref, next_ref, t2b_ref, a_ref, two_ref, out_ref, dv_ref):
    d2n = delta_ref.shape[0]
    r, _ = iotas((ROWS, LZ))
    keep = r % HB != HB - 1
    none = jnp.zeros((HB, LZ), bf16)
    for d in range(d2n + 1):
        x = delta_ref[d] if d < d2n else next_ref[...]
        up = jnp.where(keep, pltpu.roll(x.astype(f32), ROWS - 1, 0), 0.0).astype(bf16)
        for v, y in enumerate((x, up)):
            dv_ref[d, v, :, :LZ] = y
            dv_ref[d, v, :, LZ:] = jnp.concatenate([y[HB:], none], axis=0)

    def pulled(first, kd, kh):
        v = 1 if kh == 0 else 0
        lhs = jnp.concatenate([dv_ref[d + first, v] for d in range(d2n)], axis=0)
        tap = 3 * kd + kh
        return lhs, t2b_ref[2 * LZ * tap : 2 * LZ * (tap + 1)]

    deltas, planes = [], []
    for p in range(2):
        heights = (1,) if p == 0 else (2, 0)
        for even in range(2):
            depths = ((0, 2), (1, 0)) if even else ((0, 1),)
            terms = [pulled(first, kd, kh) for first, kd in depths for kh in heights]
            back = dot(
                jnp.concatenate([lhs for lhs, _ in terms], axis=1),
                jnp.concatenate([rhs for _, rhs in terms], axis=0),
            )
            here = [(p, 2 * d + 1 + even) for d in range(d2n)]
            hidden = jnp.concatenate([hh_ref[j, 2 if p else 1] for _, j in here], axis=0)
            deltas.append((back * jnp.where(hidden.astype(f32) > 0, 1.0, SLOPE)).astype(bf16))
            planes += here
    g = dot_tn(jnp.concatenate(deltas, axis=0), first_layer_columns(a_ref, planes))
    before, after = [jnp.zeros((C2, LA), f32)], [jnp.zeros((128 - C2 - 3 * C1, LA), f32)]

    def place(taps):
        return [jnp.concatenate(before + taps[i : i + 3] + after, axis=0) for i in range(0, 9, 3)]

    _, q = iotas((C1, LA))
    sums = width_sums(
        lambda tap: g[:, LA * tap : LA * (tap + 1)],
        lambda tap: jnp.where(q // CIN % 8 == tap % 8, g[:C1, LA * (9 + tap // 8) : LA * (10 + tap // 8)], 0.0),
        W1,
        C1,
        CIN,
        place,
    )
    sums = jnp.concatenate(sums, axis=0)
    out_ref[: 3 * C1] = two_ref[:, :128]
    out_ref[3 * C1 : 6 * C1] = two_ref[:, 128:256]
    out_ref[6 * C1 :] = two_ref[:, 256:] + sums


def scale_kernel(factor, sum_ref, one_ref, two_ref):
    place = (2, 0, 1)
    for tap in range(9):
        for kw in range(3):
            r, q = 3 * C1 * (tap // 4) + C1 * place[kw], C2 * (tap % 4)
            two_ref[3 * tap + kw] = sum_ref[r : r + C1, q : q + C2] * factor
            r, q = 6 * C1 + C1 * (tap // 3) + CIN * place[kw], C2 + C1 * (tap % 3)
            one_ref[3 * tap + kw] = sum_ref[r : r + CIN, q : q + C1] * factor


def gather_kernel(
    vol_hbm, cot_hbm, k1_hbm, k2_hbm, vol_ref, out_ref, k1_ref, k2_ref, cot_ref, order_ref, sems
):
    d2n = vol_ref.shape[1] // 4
    copies = [
        pltpu.make_async_copy(x, y, sems.at[i])
        for i, (x, y) in enumerate(
            [(cot_hbm, cot_ref), (vol_hbm, vol_ref), (k1_hbm, k1_ref), (k2_hbm, k2_ref)]
        )
    ]
    for copy in copies:
        copy.start()
    channels, depth, cells = cot_ref.shape
    hl = cells // 32
    r, q = iotas((WIDE, WIDE))
    order_ref[...] = one_hot(q == (r % (BLOCKS * W2)) * C2 + r // (BLOCKS * W2))
    r, q = iotas((cells, hl * 128))
    moves = [one_hot((q // 128 == r // 32) & (q % 128 == i * 32 + r % 32)) for i in range(4)]
    copies[0].wait()
    parts = [
        dot(jnp.concatenate([cot_ref[first + i] for first in range(0, channels, 4)], axis=0), moves[i])
        for i in range(4)
    ]
    together = ((parts[0] + parts[1]) + (parts[2] + parts[3])).astype(bf16)
    groups = [together[i * depth : (i + 1) * depth] for i in range(channels // 4)]
    x = jnp.concatenate(
        [jnp.concatenate([g[:, h * 128 : (h + 1) * 128] for g in groups], axis=1) for h in range(hl)], axis=0
    )
    x = dot(x, order_ref[...]).astype(bf16)
    for device in range(out_ref.shape[0]):
        for h in range(hl):
            at = h * depth + device * d2n
            out_ref[device, h * d2n : (h + 1) * d2n] = x[at : at + d2n]
    for copy in copies[1:]:
        copy.wait()


def last_planes_kernel(vol_ref, low_ref):
    low_ref[...] = vol_ref[:, vol_ref.shape[1] - 3 :]


def scatter_kernel(d2n, got_ref, out_ref):
    channels, depth, cells = out_ref.shape
    hl = cells // 32
    count = got_ref.shape[0]
    r, q = iotas((count, count))
    row, plane = travel_order(q, depth, d2n, hl)
    got = dot(one_hot(r == row * depth + plane), got_ref[...]).astype(bf16)
    r, q = iotas((hl * 128, cells))
    moves = [one_hot((r // 128 == q // 32) & (r % 128 == i * 32 + q % 32)) for i in range(4)]
    groups = channels // 4
    for g in range(groups):
        x = jnp.concatenate(
            [got[(h * groups + g) * depth : (h * groups + g + 1) * depth] for h in range(hl)], axis=1
        )
        for i in range(4):
            out_ref[4 * g + i] = dot(x, moves[i]).astype(bf16)


def call(kernel, name, outs, *args, scratch=(), apart=(), apart_out=()):
    return pl.pallas_call(
        kernel,
        name=name,
        in_specs=[pl.BlockSpec(memory_space=pltpu.HBM if i in apart else pltpu.VMEM) for i in range(len(args))],
        out_specs=[
            pl.BlockSpec(memory_space=pltpu.HBM if i in apart_out else pltpu.VMEM) for i in range(len(outs))
        ],
        out_shape=[
            pltpu.HBM(shape, dtype) if i in apart_out else jax.ShapeDtypeStruct(shape, dtype)
            for i, (shape, dtype) in enumerate(outs)
        ],
        scratch_shapes=list(scratch),
        compiler_params=pltpu.CompilerParams(vmem_limit_bytes=32 << 20),
    )(*[pltpu.with_memory_space_constraint(x, pltpu.HBM) if i in apart else x for i, x in enumerate(args)])


def passed_along(block, distance):
    devices = range(lax.axis_size("space"))
    return lax.ppermute(block, "space", [(i - distance, i) for i in devices if i - distance in devices])


def with_partner(block, bit):
    count = lax.axis_size("dp") * lax.axis_size("space")
    return lax.ppermute(block, ("dp", "space"), [(i, i ^ bit) for i in range(count)])


def total_and_exchange(terms, rows):
    devices = lax.axis_size("space")
    here = lax.axis_index("space")
    count = rows.shape[0] // devices
    blocks = rows.reshape(devices, count, 128)
    half = terms.shape[0] // 2
    first, second = rows.shape[0] // 2, rows.shape[0] // 2 + half
    even = here % 2 == 0
    bit = 1
    while bit < devices:
        mine = (here // bit) % 2 == 0
        pairs = blocks.reshape(devices // (2 * bit), 2, bit, count, 128)
        kept = jnp.where(mine, pairs[:, 0], pairs[:, 1])
        sent = jnp.where(mine, pairs[:, 1], pairs[:, 0]).reshape(first, 128)
        high = lax.reduce_precision(terms, 8, 7)
        rest = lax.reduce_precision(terms - high, 8, 7)
        if bit == 1:
            stay = jnp.where(even, terms[:half], terms[half:])
            high, rest = (jnp.where(even, x[half:], x[:half]) for x in (high, rest))
        else:
            stay = high + rest
        got = with_partner(jnp.concatenate([sent, high.astype(bf16), rest.astype(bf16)], axis=0), bit)
        terms = stay + (got[first:second].astype(f32) + got[second:].astype(f32))
        came = got[:first].reshape(kept.shape)
        blocks = jnp.where(mine, jnp.stack([kept, came], 1), jnp.stack([came, kept], 1))
        bit *= 2
    while bit < devices * lax.axis_size("dp"):
        terms = terms + with_partner(terms, bit)
        bit *= 2
    return terms, blocks.reshape(rows.shape)


def rejoined(half):
    other = with_partner(half, 1)
    even = lax.axis_index("space") % 2 == 0
    return jnp.where(even, jnp.concatenate([half, other], 0), jnp.concatenate([other, half], 0))


def local(volumes, kernel_one, kernel_two, cotangent):
    _, _, planes, height, width = volumes.shape
    d1n, d2n = planes // 2, planes // 4
    _, _, depth, cells = cotangent.shape
    vol, cot = volumes[0], cotangent[0]
    devices = lax.axis_size("space")
    travelling = depth * (cells // 32) * (C2 // 4)

    k1 = kernel_one.transpose(2, 3, 4, 1, 0).reshape(27, CIN, C1)
    k2 = kernel_two.transpose(2, 3, 4, 1, 0).reshape(27 * C1, C2)
    vol, cot_rows, k1, k2 = call(
        gather_kernel,
        "gather",
        [(vol.shape, bf16), ((devices, depth // devices * (cells // 32), WIDE), bf16), (k1.shape, bf16), (k2.shape, bf16)],
        vol,
        cot,
        k1,
        k2,
        scratch=[
            pltpu.VMEM(cot.shape, bf16),
            pltpu.VMEM((WIDE, WIDE), bf16),
            pltpu.SemaphoreType.DMA((4,)),
        ],
        apart=(0, 1, 2, 3),
    )
    (low,) = call(last_planes_kernel, "last_planes", [((CIN, 3, height, width), bf16)], vol)
    low = passed_along(low, 1)
    cot_here = lax.all_to_all(cot_rows, "space", 0, 0, tiled=True)

    a, hh, send, slope = call(
        forward_kernel,
        "forward",
        [
            ((planes + 3, 5, ROWS + HB, LA), bf16),
            ((d1n + 1, 3, ROWS, LH), bf16),
            ((travelling, 128), bf16),
            ((d2n, ROWS, LZ), bf16),
        ],
        vol,
        low,
        k1,
        k2,
        scratch=[
            pltpu.VMEM((planes + 3, 5, ROWS + HB, LA), bf16),
            pltpu.VMEM((11 * LA, LH), bf16),
            pltpu.VMEM((9 * 2 * LH, LZ), bf16),
            pltpu.SemaphoreType.DMA,
        ],
        apart_out=(0,),
    )
    (delta,) = call(delta_kernel, "delta", [((d2n, ROWS, LZ), bf16)], cot_here, slope)
    delta_next = passed_along(delta[0], -1)
    term_two, t2b, a = call(
        second_gradient_kernel,
        "second_gradient",
        [((3 * C1, 384), f32), ((9 * 2 * LZ, LH), bf16), (a.shape, bf16)],
        hh,
        delta,
        k2,
        a,
        scratch=[pltpu.SemaphoreType.DMA],
        apart=(3,),
    )
    (terms,) = call(
        first_gradient_kernel,
        "first_gradient",
        [((9 * C1, 128), f32)],
        hh,
        delta,
        delta_next,
        t2b,
        a,
        term_two,
        scratch=[pltpu.VMEM((d2n + 1, 2, ROWS, 2 * LZ), bf16)],
    )
    half, got = total_and_exchange(terms, send)
    (out,) = call(functools.partial(scatter_kernel, d2n), "scatter", [((C2, depth, cells), bf16)], got)
    half, out = lax.optimization_barrier((half, out))
    terms = rejoined(half)
    count = volumes.shape[0] * lax.axis_size("dp")
    factor = 1.0 / math.sqrt(count * depth * (height // 4) ** 2)
    one, two = call(
        functools.partial(scale_kernel, factor),
        "scale",
        [((27, CIN, C1), f32), ((27, C1, C2), f32)],
        terms,
    )
    return (
        out[None],
        one.reshape(3, 3, 3, CIN, C1).transpose(4, 3, 0, 1, 2),
        two.reshape(3, 3, 3, C1, C2).transpose(4, 3, 0, 1, 2),
    )


def solution(mesh):
    placed = (P("dp", None, "space", None, None), P(), P(), P("dp", None, None, "space"))
    return jax.shard_map(
        local,
        mesh=mesh,
        in_specs=placed,
        out_specs=(P("dp", None, None, "space"), P(), P()),
        check_vma=False,
    )
```

```python
import functools
import math

import jax
import jax.numpy as jnp
from jax import lax
from jax.experimental import pallas as pl
from jax.experimental.pallas import tpu as pltpu
from jax.sharding import PartitionSpec as P

f32 = jnp.float32
bf16 = jnp.bfloat16

SLOPE = 0.3
BLOCKS = 4
HB = 32
CIN, C1, C2 = 4, 16, 32
W0, W1, W2 = 32, 16, 8
ROWS = BLOCKS * HB
LA, LH, LZ = W0 * CIN, W1 * C1, W2 * C2
EDGE = LA // BLOCKS
WIDE = BLOCKS * LZ
TAPS = [(kd, kh) for kd in range(3) for kh in range(3)]
INPUT_ROWS = {(0, 0): 4, (0, 1): 0, (0, 2): 1, (1, 0): 1, (1, 1): 2, (1, 2): 3}


def dot(a, b):
    return jnp.dot(a, b, preferred_element_type=f32)


def dot_nt(a, b):
    return lax.dot_general(a, b, (((1,), (1,)), ((), ())), preferred_element_type=f32)


def dot_tn(a, b):
    return lax.dot_general(a, b, (((0,), (0,)), ((), ())), preferred_element_type=f32)


def exact_nt(a, b):
    return lax.dot_general(
        a, b, (((1,), (1,)), ((), ())), precision=lax.Precision.HIGHEST, preferred_element_type=f32
    )


def iotas(shape):
    rows, lanes = shape
    return lax.broadcasted_iota(jnp.int32, (rows, 1), 0), lax.broadcasted_iota(jnp.int32, (1, lanes), 1)


def one_hot(mask):
    return jnp.where(mask, 1.0, 0.0).astype(bf16)


def width_order():
    r, q = iotas((CIN * 128, (CIN + 1) * 128))
    own = (q % CIN) * 128 + (q // LA) * W0 + (q // CIN) % W0
    edge = (q % CIN) * 128 + (q % LA) // EDGE * W0 - 1
    return one_hot(r == jnp.where(q < CIN * 128, own, jnp.where(q % LA < EDGE, -1, edge)))


def height_order():
    r, q = iotas((5 * HB, 4 * HB))
    return one_hot(q == 4 * (r % HB) + jnp.where(r // HB == 4, -1, r // HB))


def channel_order():
    r, q = iotas((WIDE, WIDE))
    cells = BLOCKS * W2
    return one_hot(r == (q % cells) * C2 + q // cells)


def arrange_planes(planes, count, put):
    x = jnp.concatenate([planes(c) for c in range(CIN)], axis=1)
    y = dot(x, width_order()).astype(bf16)
    order = height_order()
    for d in range(count):
        z = dot(order, y[d * 128 : (d + 1) * 128]).astype(bf16)
        for v in range(5):
            put(d, v, [z[v * HB : (v + 1) * HB, b * LA : (b + 1) * LA] for b in range(BLOCKS + 1)])


def with_before(x):
    return jnp.concatenate([x, jnp.concatenate([jnp.zeros_like(x[:HB]), x[:-HB]], axis=0)], axis=1)


def first_layer_columns(a_ref, planes):
    _, q = iotas((HB, LA))
    times = [one_hot(q // CIN % 8 == t) for t in range(8)]
    blocks = [one_hot(q // EDGE == b) for b in range(BLOCKS)]
    cols = [[] for _ in range(11)]
    for p, j in planes:
        x = [a_ref[2 * j + kd, INPUT_ROWS[p, kh]] for kd, kh in TAPS]
        edges = [y[ROWS:] for y in x]
        eight = edges[0] * times[0]
        for t in range(1, 8):
            eight = eight + edges[t] * times[t]
        x = [y[:ROWS] for y in x]
        for y in (eight, edges[8] * times[0]):
            x.append(jnp.concatenate([y * m for m in blocks], axis=0))
        for col, y in zip(cols, x):
            col.append(y)
    return jnp.concatenate([jnp.concatenate(col, axis=0) for col in cols], axis=1)


def band(taps, rows, cin, cols, cout, put):
    r, q = iotas((rows, cols))
    w, o = r // cin, q // cout
    rel = w - 2 * o + 1
    last = (w == rows // cin - 1) & (o == 0)
    for tap in range(9):
        e = [taps(3 * tap + kw) for kw in range(3)]
        own = jnp.where(rel == 0, e[0], jnp.where(rel == 1, e[1], jnp.where(rel == 2, e[2], 0.0)))
        put(tap, own.astype(bf16), jnp.where(last, e[0], 0.0).astype(bf16))


def band_back(taps, rows, cout, cols, cin, put):
    r, q = iotas((rows, cols))
    w, o = q // cin, r // cout
    rel = w - 2 * o + 1
    last = (w == cols // cin - 1) & (o == 0)
    for tap in range(9):
        e = [taps(3 * tap + kw) for kw in range(3)]
        own = jnp.where(rel == 0, e[0], jnp.where(rel == 1, e[1], jnp.where(rel == 2, e[2], 0.0)))
        put(tap, own.astype(bf16), jnp.where(last, e[0], 0.0).astype(bf16))


def spread(k, cols):
    c, q = iotas((k.shape[1], cols))
    return dot(k, one_hot(q % k.shape[1] == c))


def spread_back(k2):
    r, q = iotas((C2, C2))
    flipped = dot_nt(one_hot(r == q), k2).astype(bf16)
    flipped = jnp.concatenate([flipped, jnp.zeros((C2, 512 - 27 * C1), bf16)], axis=1)
    stacked = jnp.concatenate([flipped[:, 128 * i : 128 * (i + 1)] for i in range(4)], axis=0)
    r, q = iotas((128, LH))
    parts = [dot(stacked, one_hot((r // C1 == g) & (q % C1 == r % C1))) for g in range(8)]
    return lambda t: parts[t % 8][C2 * (t // 8) : C2 * (t // 8 + 1)]


def shifted_down(x, keep):
    return jnp.where(keep, pltpu.roll(x.astype(f32), 1, 0), 0.0).astype(bf16)


def travel_order(r, depth, d2n, hl):
    groups = hl * C2 // 4
    return (r // d2n) % groups, r // (groups * d2n) * d2n + r % d2n


def by_height(r, d2n):
    group, plane, h2 = r // (d2n * HB), (r // HB) % d2n, r % HB
    return (h2 * (C2 // 4) + group) * d2n + plane


def puts(ref, half):
    def put(tap, own, other):
        ref[2 * half * tap : 2 * half * tap + half] = own
        ref[2 * half * tap + half : 2 * half * (tap + 1)] = other

    return put


def tiled(each, times):
    return lambda t: jnp.concatenate([each(t)] * times, axis=0)


def forward_kernel(
    vol_ref, low_ref, k1_ref, k2_ref, a_hbm, hh_ref, send_ref, slope_ref, a_ref, t1_ref, t2_ref, sem
):
    count = vol_ref.shape[1]
    planes = hh_ref.shape[0]
    d2n = slope_ref.shape[0]
    copy = pltpu.make_async_copy(a_ref, a_hbm, sem)

    def put_from(first):
        def put(d, v, blocks):
            for b, x in enumerate(blocks):
                a_ref[first + d, v, b * HB : (b + 1) * HB] = x

        return put

    k1 = jnp.concatenate([k1_ref[t].astype(f32) for t in range(27) for _ in range(16 // CIN)], axis=0)
    k1 = spread(k1.astype(bf16), LH)
    def put_own(tap, own, _):
        t1_ref[LA * tap : LA * (tap + 1)] = own

    band(tiled(lambda t: k1[16 * t : 16 * (t + 1)], LA // 16), LA, CIN, LH, C1, put_own)
    _, q = iotas((LA, LH))
    for i, taps in enumerate((range(8), [8] * 8)):
        edge = jnp.concatenate([k1[48 * t : 48 * t + CIN] for _ in range(BLOCKS) for t in taps], axis=0)
        t1_ref[LA * (9 + i) : LA * (10 + i)] = jnp.where(q < C1, edge, 0.0).astype(bf16)
    k2 = spread(k2_ref[...], LZ)
    band(tiled(lambda t: k2[C1 * t : C1 * (t + 1)], W1), LH, C1, LZ, C2, puts(t2_ref, LH))
    arrange_planes(lambda c: low_ref[c].reshape(3 * 128, 128), 3, put_from(0))
    arrange_planes(lambda c: vol_ref[c].reshape(count * 128, 128), count, put_from(3))
    copy.start()

    r, _ = iotas((planes * ROWS, LH))
    keep = r % HB != 0
    for p in range(2):
        linear = dot(first_layer_columns(a_ref, [(p, j) for j in range(planes)]), t1_ref[...])
        hidden = jnp.where(linear > 0, linear, SLOPE * linear).astype(bf16)
        variants = [(1, hidden)] if p == 0 else [(2, hidden), (0, shifted_down(hidden, keep))]
        for v, x in variants:
            for j in range(planes):
                hh_ref[j, v] = x[j * ROWS : (j + 1) * ROWS]

    linear = dot(second_layer_columns(hh_ref, d2n), t2_ref[...])
    out = jnp.where(linear > 0, linear, SLOPE * linear).astype(bf16)
    positive = jnp.where(linear > 0, 1.0, 0.0).astype(bf16)
    for d in range(d2n):
        slope_ref[d] = positive[d * ROWS : (d + 1) * ROWS]
    wide = jnp.concatenate(
        [
            jnp.concatenate([out[d * ROWS + b * HB : d * ROWS + (b + 1) * HB] for b in range(BLOCKS)], axis=1)
            for d in range(d2n)
        ],
        axis=0,
    )
    groups = C2 // 4
    by_channel = dot(wide, channel_order()).astype(bf16)
    stacked = jnp.concatenate([by_channel[:, 128 * g : 128 * (g + 1)] for g in range(groups)], axis=0)
    r, q = iotas((stacked.shape[0], stacked.shape[0]))
    send_ref[...] = dot(one_hot(r == by_height(q, d2n)), stacked).astype(bf16)
    copy.wait()


def second_layer_columns(hh_ref, d2n):
    cols = [jnp.concatenate([with_before(hh_ref[2 * d + kd, kh]) for d in range(d2n)], axis=0) for kd, kh in TAPS]
    return jnp.concatenate(cols, axis=1)


def delta_kernel(cot_ref, slope_ref, delta_ref):
    d2n = delta_ref.shape[0]
    devices, lines, _ = cot_ref.shape
    hl = lines // d2n
    r, q = iotas((d2n * HB, devices * lines))
    plane, h2 = r // HB, r % HB
    order = one_hot(q == h2 // hl * lines + h2 % hl * d2n + plane)
    got = dot(order, jnp.concatenate([cot_ref[i] for i in range(devices)], axis=0))
    for d in range(d2n):
        for b in range(BLOCKS):
            c = got[d * HB : (d + 1) * HB, b * LZ : (b + 1) * LZ]
            slope = jnp.where(slope_ref[d, b * HB : (b + 1) * HB].astype(f32) > 0, 1.0, SLOPE)
            delta_ref[d, b * HB : (b + 1) * HB] = (c * slope).astype(bf16)


def diagonals(x, before, cells, cout, cin):
    lanes = 2 * cells * cin
    _, q = iotas((cout, lanes))
    w = q // cin
    ahead = jnp.zeros((cout, lanes), f32)
    behind = jnp.zeros((cout, lanes), f32)
    for o in range(cells):
        y = x[o * cout : (o + 1) * cout]
        ahead = jnp.where(w // 2 == o, y, ahead)
        if o:
            behind = jnp.where(w == 2 * o - 1, y, behind)
    return ahead, behind + before


def width_sums(own, before, cells, cout, cin, place):
    lanes = 2 * cells * cin
    both = [diagonals(own(tap), before(tap), cells, cout, cin) for tap in range(9)]
    ahead, behind = place([x for x, _ in both]), place([x for _, x in both])
    r, q = iotas((2 * cin, lanes))
    pick = jnp.where((q // cin % 2 == r // cin) & (q % cin == r % cin), 1.0, 0.0)
    r, q = iotas((max(cin, 8), lanes))
    every = jnp.where(q % cin == r, 1.0, 0.0)
    return [jnp.concatenate([exact_nt(pick, x), exact_nt(every, y)], axis=0) for x, y in zip(ahead, behind)]


def second_gradient_kernel(hh_ref, delta_ref, k2_ref, a_hbm, out_ref, t2b_ref, a_ref, sem):
    copy = pltpu.make_async_copy(a_hbm, a_ref, sem)
    copy.start()
    d2n = delta_ref.shape[0]
    delta = jnp.concatenate([delta_ref[d] for d in range(d2n)], axis=0)
    g = dot_tn(delta, second_layer_columns(hh_ref, d2n))
    none = [jnp.zeros((3 * C2, LH), f32)]
    _, q = iotas((C2, LH))
    (sums,) = width_sums(
        lambda tap: g[:, 2 * LH * tap : 2 * LH * tap + LH],
        lambda tap: jnp.where(q // C1 == W1 - 1, g[:C2, 2 * LH * tap + LH : 2 * LH * (tap + 1)], 0.0),
        W2,
        C2,
        C1,
        lambda taps: [jnp.concatenate(taps + none, axis=0)],
    )
    out_ref[...] = sums
    band_back(tiled(spread_back(k2_ref[...]), W2), LZ, C2, LH, C1, puts(t2b_ref, LZ))
    copy.wait()


def first_gradient_kernel(hh_ref, delta_ref, next_ref, t2b_ref, a_ref, two_ref, out_ref, dv_ref):
    d2n = delta_ref.shape[0]
    r, _ = iotas((ROWS, LZ))
    keep = r % HB != HB - 1
    none = jnp.zeros((HB, LZ), bf16)
    for d in range(d2n + 1):
        x = delta_ref[d] if d < d2n else next_ref[...]
        up = jnp.where(keep, pltpu.roll(x.astype(f32), ROWS - 1, 0), 0.0).astype(bf16)
        for v, y in enumerate((x, up)):
            dv_ref[d, v, :, :LZ] = y
            dv_ref[d, v, :, LZ:] = jnp.concatenate([y[HB:], none], axis=0)

    def pulled(first, kd, kh):
        v = 1 if kh == 0 else 0
        lhs = jnp.concatenate([dv_ref[d + first, v] for d in range(d2n)], axis=0)
        tap = 3 * kd + kh
        return lhs, t2b_ref[2 * LZ * tap : 2 * LZ * (tap + 1)]

    deltas, planes = [], []
    for p in range(2):
        heights = (1,) if p == 0 else (2, 0)
        for even in range(2):
            depths = ((0, 2), (1, 0)) if even else ((0, 1),)
            terms = [pulled(first, kd, kh) for first, kd in depths for kh in heights]
            back = dot(
                jnp.concatenate([lhs for lhs, _ in terms], axis=1),
                jnp.concatenate([rhs for _, rhs in terms], axis=0),
            )
            here = [(p, 2 * d + 1 + even) for d in range(d2n)]
            hidden = jnp.concatenate([hh_ref[j, 2 if p else 1] for _, j in here], axis=0)
            deltas.append((back * jnp.where(hidden.astype(f32) > 0, 1.0, SLOPE)).astype(bf16))
            planes += here
    g = dot_tn(jnp.concatenate(deltas, axis=0), first_layer_columns(a_ref, planes))
    before, after = [jnp.zeros((C2, LA), f32)], [jnp.zeros((128 - C2 - 3 * C1, LA), f32)]

    def place(taps):
        return [jnp.concatenate(before + taps[i : i + 3] + after, axis=0) for i in range(0, 9, 3)]

    _, q = iotas((C1, LA))
    sums = width_sums(
        lambda tap: g[:, LA * tap : LA * (tap + 1)],
        lambda tap: jnp.where(q // CIN % 8 == tap % 8, g[:C1, LA * (9 + tap // 8) : LA * (10 + tap // 8)], 0.0),
        W1,
        C1,
        CIN,
        place,
    )
    sums = jnp.concatenate(sums, axis=0)
    out_ref[: 3 * C1] = two_ref[:, :128]
    out_ref[3 * C1 : 6 * C1] = two_ref[:, 128:256]
    out_ref[6 * C1 :] = two_ref[:, 256:] + sums


def scale_kernel(factor, sum_ref, one_ref, two_ref):
    place = (2, 0, 1)
    for tap in range(9):
        for kw in range(3):
            r, q = 3 * C1 * (tap // 4) + C1 * place[kw], C2 * (tap % 4)
            two_ref[3 * tap + kw] = sum_ref[r : r + C1, q : q + C2] * factor
            r, q = 6 * C1 + C1 * (tap // 3) + CIN * place[kw], C2 + C1 * (tap % 3)
            one_ref[3 * tap + kw] = sum_ref[r : r + CIN, q : q + C1] * factor


def gather_kernel(
    vol_hbm, cot_hbm, k1_hbm, k2_hbm, vol_ref, out_ref, k1_ref, k2_ref, cot_ref, order_ref, sems
):
    d2n = vol_ref.shape[1] // 4
    copies = [
        pltpu.make_async_copy(x, y, sems.at[i])
        for i, (x, y) in enumerate(
            [(cot_hbm, cot_ref), (vol_hbm, vol_ref), (k1_hbm, k1_ref), (k2_hbm, k2_ref)]
        )
    ]
    for copy in copies:
        copy.start()
    channels, depth, cells = cot_ref.shape
    hl = cells // 32
    r, q = iotas((WIDE, WIDE))
    order_ref[...] = one_hot(q == (r % (BLOCKS * W2)) * C2 + r // (BLOCKS * W2))
    r, q = iotas((cells, hl * 128))
    moves = [one_hot((q // 128 == r // 32) & (q % 128 == i * 32 + r % 32)) for i in range(4)]
    copies[0].wait()
    parts = [
        dot(jnp.concatenate([cot_ref[first + i] for first in range(0, channels, 4)], axis=0), moves[i])
        for i in range(4)
    ]
    together = ((parts[0] + parts[1]) + (parts[2] + parts[3])).astype(bf16)
    groups = [together[i * depth : (i + 1) * depth] for i in range(channels // 4)]
    x = jnp.concatenate(
        [jnp.concatenate([g[:, h * 128 : (h + 1) * 128] for g in groups], axis=1) for h in range(hl)], axis=0
    )
    x = dot(x, order_ref[...]).astype(bf16)
    for device in range(out_ref.shape[0]):
        for h in range(hl):
            at = h * depth + device * d2n
            out_ref[device, h * d2n : (h + 1) * d2n] = x[at : at + d2n]
    for copy in copies[1:]:
        copy.wait()


def last_planes_kernel(vol_ref, low_ref):
    low_ref[...] = vol_ref[:, vol_ref.shape[1] - 3 :]


def scatter_kernel(d2n, got_ref, out_ref):
    channels, depth, cells = out_ref.shape
    hl = cells // 32
    count = got_ref.shape[0]
    r, q = iotas((count, count))
    row, plane = travel_order(q, depth, d2n, hl)
    got = dot(one_hot(r == row * depth + plane), got_ref[...]).astype(bf16)
    r, q = iotas((hl * 128, cells))
    moves = [one_hot((r // 128 == q // 32) & (r % 128 == i * 32 + q % 32)) for i in range(4)]
    groups = channels // 4
    for g in range(groups):
        x = jnp.concatenate(
            [got[(h * groups + g) * depth : (h * groups + g + 1) * depth] for h in range(hl)], axis=1
        )
        for i in range(4):
            out_ref[4 * g + i] = dot(x, moves[i]).astype(bf16)


def call(kernel, name, outs, *args, scratch=(), apart=(), apart_out=()):
    return pl.pallas_call(
        kernel,
        name=name,
        in_specs=[pl.BlockSpec(memory_space=pltpu.HBM if i in apart else pltpu.VMEM) for i in range(len(args))],
        out_specs=[
            pl.BlockSpec(memory_space=pltpu.HBM if i in apart_out else pltpu.VMEM) for i in range(len(outs))
        ],
        out_shape=[
            pltpu.HBM(shape, dtype) if i in apart_out else jax.ShapeDtypeStruct(shape, dtype)
            for i, (shape, dtype) in enumerate(outs)
        ],
        scratch_shapes=list(scratch),
        compiler_params=pltpu.CompilerParams(vmem_limit_bytes=32 << 20),
    )(*[pltpu.with_memory_space_constraint(x, pltpu.HBM) if i in apart else x for i, x in enumerate(args)])


def passed_along(block, distance):
    devices = range(lax.axis_size("space"))
    return lax.ppermute(block, "space", [(i - distance, i) for i in devices if i - distance in devices])


def with_partner(block, bit):
    count = lax.axis_size("dp") * lax.axis_size("space")
    return lax.ppermute(block, ("dp", "space"), [(i, i ^ bit) for i in range(count)])


def total_and_exchange(terms, rows):
    devices = lax.axis_size("space")
    here = lax.axis_index("space")
    count = rows.shape[0] // devices
    blocks = rows.reshape(devices, count, 128)
    half = terms.shape[0] // 2
    first, second = rows.shape[0] // 2, rows.shape[0] // 2 + half
    even = here % 2 == 0
    bit = 1
    while bit < devices:
        mine = (here // bit) % 2 == 0
        pairs = blocks.reshape(devices // (2 * bit), 2, bit, count, 128)
        kept = jnp.where(mine, pairs[:, 0], pairs[:, 1])
        sent = jnp.where(mine, pairs[:, 1], pairs[:, 0]).reshape(first, 128)
        high = lax.reduce_precision(terms, 8, 7)
        rest = lax.reduce_precision(terms - high, 8, 7)
        if bit == 1:
            stay = jnp.where(even, terms[:half], terms[half:])
            high, rest = (jnp.where(even, x[half:], x[:half]) for x in (high, rest))
        else:
            stay = high + rest
        got = with_partner(jnp.concatenate([sent, high.astype(bf16), rest.astype(bf16)], axis=0), bit)
        terms = stay + (got[first:second].astype(f32) + got[second:].astype(f32))
        came = got[:first].reshape(kept.shape)
        blocks = jnp.where(mine, jnp.stack([kept, came], 1), jnp.stack([came, kept], 1))
        bit *= 2
    while 2 * bit < devices * lax.axis_size("dp"):
        terms = terms + with_partner(terms, bit)
        bit *= 2
    beyond = [with_partner(terms, mask) for mask in (bit, 1, bit ^ 1)]
    return terms, beyond, blocks.reshape(rows.shape)


def rejoined(terms, beyond):
    mine, other = terms + beyond[0], beyond[1] + beyond[2]
    even = lax.axis_index("space") % 2 == 0
    return jnp.where(even, jnp.concatenate([mine, other], 0), jnp.concatenate([other, mine], 0))


def local(volumes, kernel_one, kernel_two, cotangent):
    _, _, planes, height, width = volumes.shape
    d1n, d2n = planes // 2, planes // 4
    _, _, depth, cells = cotangent.shape
    vol, cot = volumes[0], cotangent[0]
    devices = lax.axis_size("space")
    travelling = depth * (cells // 32) * (C2 // 4)

    k1 = kernel_one.transpose(2, 3, 4, 1, 0).reshape(27, CIN, C1)
    k2 = kernel_two.transpose(2, 3, 4, 1, 0).reshape(27 * C1, C2)
    vol, cot_rows, k1, k2 = call(
        gather_kernel,
        "gather",
        [(vol.shape, bf16), ((devices, depth // devices * (cells // 32), WIDE), bf16), (k1.shape, bf16), (k2.shape, bf16)],
        vol,
        cot,
        k1,
        k2,
        scratch=[
            pltpu.VMEM(cot.shape, bf16),
            pltpu.VMEM((WIDE, WIDE), bf16),
            pltpu.SemaphoreType.DMA((4,)),
        ],
        apart=(0, 1, 2, 3),
    )
    (low,) = call(last_planes_kernel, "last_planes", [((CIN, 3, height, width), bf16)], vol)
    low = passed_along(low, 1)
    cot_here = lax.all_to_all(cot_rows, "space", 0, 0, tiled=True)

    a, hh, send, slope = call(
        forward_kernel,
        "forward",
        [
            ((planes + 3, 5, ROWS + HB, LA), bf16),
            ((d1n + 1, 3, ROWS, LH), bf16),
            ((travelling, 128), bf16),
            ((d2n, ROWS, LZ), bf16),
        ],
        vol,
        low,
        k1,
        k2,
        scratch=[
            pltpu.VMEM((planes + 3, 5, ROWS + HB, LA), bf16),
            pltpu.VMEM((11 * LA, LH), bf16),
            pltpu.VMEM((9 * 2 * LH, LZ), bf16),
            pltpu.SemaphoreType.DMA,
        ],
        apart_out=(0,),
    )
    (delta,) = call(delta_kernel, "delta", [((d2n, ROWS, LZ), bf16)], cot_here, slope)
    delta_next = passed_along(delta[0], -1)
    term_two, t2b, a = call(
        second_gradient_kernel,
        "second_gradient",
        [((3 * C1, 384), f32), ((9 * 2 * LZ, LH), bf16), (a.shape, bf16)],
        hh,
        delta,
        k2,
        a,
        scratch=[pltpu.SemaphoreType.DMA],
        apart=(3,),
    )
    (terms,) = call(
        first_gradient_kernel,
        "first_gradient",
        [((9 * C1, 128), f32)],
        hh,
        delta,
        delta_next,
        t2b,
        a,
        term_two,
        scratch=[pltpu.VMEM((d2n + 1, 2, ROWS, 2 * LZ), bf16)],
    )
    terms, beyond, got = total_and_exchange(terms, send)
    (out,) = call(functools.partial(scatter_kernel, d2n), "scatter", [((C2, depth, cells), bf16)], got)
    terms = rejoined(terms, beyond)
    count = volumes.shape[0] * lax.axis_size("dp")
    factor = 1.0 / math.sqrt(count * depth * (height // 4) ** 2)
    one, two = call(
        functools.partial(scale_kernel, factor),
        "scale",
        [((27, CIN, C1), f32), ((27, C1, C2), f32)],
        terms,
    )
    return (
        out[None],
        one.reshape(3, 3, 3, CIN, C1).transpose(4, 3, 0, 1, 2),
        two.reshape(3, 3, 3, C1, C2).transpose(4, 3, 0, 1, 2),
    )


def solution(mesh):
    placed = (P("dp", None, "space", None, None), P(), P(), P("dp", None, None, "space"))
    return jax.shard_map(
        local,
        mesh=mesh,
        in_specs=placed,
        out_specs=(P("dp", None, None, "space"), P(), P()),
        check_vma=False,
    )
```

```python
import functools
import math

import jax
import jax.numpy as jnp
from jax import lax
from jax.experimental import pallas as pl
from jax.experimental.pallas import tpu as pltpu
from jax.sharding import PartitionSpec as P

f32 = jnp.float32
bf16 = jnp.bfloat16

SLOPE = 0.3
BLOCKS = 4
HB = 32
CIN, C1, C2 = 4, 16, 32
W0, W1, W2 = 32, 16, 8
ROWS = BLOCKS * HB
LA, LH, LZ = W0 * CIN, W1 * C1, W2 * C2
EDGE = LA // BLOCKS
WIDE = BLOCKS * LZ
TAPS = [(kd, kh) for kd in range(3) for kh in range(3)]
INPUT_ROWS = {(0, 0): 4, (0, 1): 0, (0, 2): 1, (1, 0): 1, (1, 1): 2, (1, 2): 3}


def dot(a, b):
    return jnp.dot(a, b, preferred_element_type=f32)


def dot_nt(a, b):
    return lax.dot_general(a, b, (((1,), (1,)), ((), ())), preferred_element_type=f32)


def dot_tn(a, b):
    return lax.dot_general(a, b, (((0,), (0,)), ((), ())), preferred_element_type=f32)


def exact_nt(a, b):
    a = a.astype(bf16)
    total = None
    for _ in range(3):
        part = b.astype(bf16)
        b = b - part.astype(f32)
        total = dot_nt(a, part) if total is None else total + dot_nt(a, part)
    return total


def iotas(shape):
    rows, lanes = shape
    return lax.broadcasted_iota(jnp.int32, (rows, 1), 0), lax.broadcasted_iota(jnp.int32, (1, lanes), 1)


def one_hot(mask):
    return jnp.where(mask, 1.0, 0.0).astype(bf16)


def width_order():
    r, q = iotas((CIN * 128, (CIN + 1) * 128))
    own = (q % CIN) * 128 + (q // LA) * W0 + (q // CIN) % W0
    edge = (q % CIN) * 128 + (q % LA) // EDGE * W0 - 1
    return one_hot(r == jnp.where(q < CIN * 128, own, jnp.where(q % LA < EDGE, -1, edge)))


def height_order():
    r, q = iotas((5 * HB, 4 * HB))
    return one_hot(q == 4 * (r % HB) + jnp.where(r // HB == 4, -1, r // HB))


def channel_order():
    r, q = iotas((WIDE, WIDE))
    cells = BLOCKS * W2
    return one_hot(r == (q % cells) * C2 + q // cells)


def arrange_planes(planes, count, put):
    x = jnp.concatenate([planes(c) for c in range(CIN)], axis=1)
    y = dot(x, width_order()).astype(bf16)
    order = height_order()
    for d in range(count):
        z = dot(order, y[d * 128 : (d + 1) * 128]).astype(bf16)
        for v in range(5):
            put(d, v, [z[v * HB : (v + 1) * HB, b * LA : (b + 1) * LA] for b in range(BLOCKS + 1)])


def with_before(x):
    return jnp.concatenate([x, jnp.concatenate([jnp.zeros_like(x[:HB]), x[:-HB]], axis=0)], axis=1)


def first_layer_columns(a_ref, planes):
    _, q = iotas((HB, LA))
    times = [one_hot(q // CIN % 8 == t) for t in range(8)]
    blocks = [one_hot(q // EDGE == b) for b in range(BLOCKS)]
    cols = [[] for _ in range(11)]
    for p, j in planes:
        x = [a_ref[2 * j + kd, INPUT_ROWS[p, kh]] for kd, kh in TAPS]
        edges = [y[ROWS:] for y in x]
        eight = edges[0] * times[0]
        for t in range(1, 8):
            eight = eight + edges[t] * times[t]
        x = [y[:ROWS] for y in x]
        for y in (eight, edges[8] * times[0]):
            x.append(jnp.concatenate([y * m for m in blocks], axis=0))
        for col, y in zip(cols, x):
            col.append(y)
    return jnp.concatenate([jnp.concatenate(col, axis=0) for col in cols], axis=1)


def band(taps, rows, cin, cols, cout, put):
    r, q = iotas((rows, cols))
    w, o = r // cin, q // cout
    rel = w - 2 * o + 1
    last = (w == rows // cin - 1) & (o == 0)
    for tap in range(9):
        e = [taps(3 * tap + kw) for kw in range(3)]
        own = jnp.where(rel == 0, e[0], jnp.where(rel == 1, e[1], jnp.where(rel == 2, e[2], 0.0)))
        put(tap, own.astype(bf16), jnp.where(last, e[0], 0.0).astype(bf16))


def band_back(taps, rows, cout, cols, cin, put):
    r, q = iotas((rows, cols))
    w, o = q // cin, r // cout
    rel = w - 2 * o + 1
    last = (w == cols // cin - 1) & (o == 0)
    for tap in range(9):
        e = [taps(3 * tap + kw) for kw in range(3)]
        own = jnp.where(rel == 0, e[0], jnp.where(rel == 1, e[1], jnp.where(rel == 2, e[2], 0.0)))
        put(tap, own.astype(bf16), jnp.where(last, e[0], 0.0).astype(bf16))


def spread(k, cols):
    c, q = iotas((k.shape[1], cols))
    return dot(k, one_hot(q % k.shape[1] == c))


def spread_back(k2):
    r, q = iotas((C2, C2))
    flipped = dot_nt(one_hot(r == q), k2).astype(bf16)
    flipped = jnp.concatenate([flipped, jnp.zeros((C2, 512 - 27 * C1), bf16)], axis=1)
    stacked = jnp.concatenate([flipped[:, 128 * i : 128 * (i + 1)] for i in range(4)], axis=0)
    r, q = iotas((128, LH))
    parts = [dot(stacked, one_hot((r // C1 == g) & (q % C1 == r % C1))) for g in range(8)]
    return lambda t: parts[t % 8][C2 * (t // 8) : C2 * (t // 8 + 1)]


def shifted_down(x, keep):
    return jnp.where(keep, pltpu.roll(x.astype(f32), 1, 0), 0.0).astype(bf16)


def travel_order(r, depth, d2n, hl):
    groups = hl * C2 // 4
    return (r // d2n) % groups, r // (groups * d2n) * d2n + r % d2n


def by_height(r, d2n):
    group, plane, h2 = r // (d2n * HB), (r // HB) % d2n, r % HB
    return (h2 * (C2 // 4) + group) * d2n + plane


def puts(ref, half):
    def put(tap, own, other):
        ref[2 * half * tap : 2 * half * tap + half] = own
        ref[2 * half * tap + half : 2 * half * (tap + 1)] = other

    return put


def tiled(each, times):
    return lambda t: jnp.concatenate([each(t)] * times, axis=0)


def forward_kernel(
    vol_ref, low_ref, k1_ref, k2_ref, a_hbm, hh_ref, send_ref, slope_ref, a_ref, t1_ref, t2_ref, sem
):
    count = vol_ref.shape[1]
    planes = hh_ref.shape[0]
    d2n = slope_ref.shape[0]
    copy = pltpu.make_async_copy(a_ref, a_hbm, sem)

    def put_from(first):
        def put(d, v, blocks):
            for b, x in enumerate(blocks):
                a_ref[first + d, v, b * HB : (b + 1) * HB] = x

        return put

    k1 = jnp.concatenate([k1_ref[t].astype(f32) for t in range(27) for _ in range(16 // CIN)], axis=0)
    k1 = spread(k1.astype(bf16), LH)
    def put_own(tap, own, _):
        t1_ref[LA * tap : LA * (tap + 1)] = own

    band(tiled(lambda t: k1[16 * t : 16 * (t + 1)], LA // 16), LA, CIN, LH, C1, put_own)
    _, q = iotas((LA, LH))
    for i, taps in enumerate((range(8), [8] * 8)):
        edge = jnp.concatenate([k1[48 * t : 48 * t + CIN] for _ in range(BLOCKS) for t in taps], axis=0)
        t1_ref[LA * (9 + i) : LA * (10 + i)] = jnp.where(q < C1, edge, 0.0).astype(bf16)
    k2 = spread(k2_ref[...], LZ)
    band(tiled(lambda t: k2[C1 * t : C1 * (t + 1)], W1), LH, C1, LZ, C2, puts(t2_ref, LH))
    arrange_planes(lambda c: low_ref[c].reshape(3 * 128, 128), 3, put_from(0))
    arrange_planes(lambda c: vol_ref[c].reshape(count * 128, 128), count, put_from(3))
    copy.start()

    r, _ = iotas((planes * ROWS, LH))
    keep = r % HB != 0
    for p in range(2):
        linear = dot(first_layer_columns(a_ref, [(p, j) for j in range(planes)]), t1_ref[...])
        hidden = jnp.where(linear > 0, linear, SLOPE * linear).astype(bf16)
        variants = [(1, hidden)] if p == 0 else [(2, hidden), (0, shifted_down(hidden, keep))]
        for v, x in variants:
            for j in range(planes):
                hh_ref[j, v] = x[j * ROWS : (j + 1) * ROWS]

    linear = dot(second_layer_columns(hh_ref, d2n), t2_ref[...])
    out = jnp.where(linear > 0, linear, SLOPE * linear).astype(bf16)
    positive = jnp.where(linear > 0, 1.0, 0.0).astype(bf16)
    for d in range(d2n):
        slope_ref[d] = positive[d * ROWS : (d + 1) * ROWS]
    wide = jnp.concatenate(
        [
            jnp.concatenate([out[d * ROWS + b * HB : d * ROWS + (b + 1) * HB] for b in range(BLOCKS)], axis=1)
            for d in range(d2n)
        ],
        axis=0,
    )
    groups = C2 // 4
    by_channel = dot(wide, channel_order()).astype(bf16)
    stacked = jnp.concatenate([by_channel[:, 128 * g : 128 * (g + 1)] for g in range(groups)], axis=0)
    r, q = iotas((stacked.shape[0], stacked.shape[0]))
    send_ref[...] = dot(one_hot(r == by_height(q, d2n)), stacked).astype(bf16)
    copy.wait()


def second_layer_columns(hh_ref, d2n):
    cols = [jnp.concatenate([with_before(hh_ref[2 * d + kd, kh]) for d in range(d2n)], axis=0) for kd, kh in TAPS]
    return jnp.concatenate(cols, axis=1)


def delta_kernel(cot_ref, slope_ref, delta_ref):
    d2n = delta_ref.shape[0]
    devices, lines, _ = cot_ref.shape
    hl = lines // d2n
    r, q = iotas((d2n * HB, devices * lines))
    plane, h2 = r // HB, r % HB
    order = one_hot(q == h2 // hl * lines + h2 % hl * d2n + plane)
    got = dot(order, jnp.concatenate([cot_ref[i] for i in range(devices)], axis=0))
    for d in range(d2n):
        for b in range(BLOCKS):
            c = got[d * HB : (d + 1) * HB, b * LZ : (b + 1) * LZ]
            slope = jnp.where(slope_ref[d, b * HB : (b + 1) * HB].astype(f32) > 0, 1.0, SLOPE)
            delta_ref[d, b * HB : (b + 1) * HB] = (c * slope).astype(bf16)


def diagonals(x, before, cells, cout, cin):
    lanes = 2 * cells * cin
    _, q = iotas((cout, lanes))
    w = q // cin
    ahead = jnp.zeros((cout, lanes), f32)
    behind = jnp.zeros((cout, lanes), f32)
    for o in range(cells):
        y = x[o * cout : (o + 1) * cout]
        ahead = jnp.where(w // 2 == o, y, ahead)
        if o:
            behind = jnp.where(w == 2 * o - 1, y, behind)
    return ahead, behind + before


def width_sums(own, before, cells, cout, cin, place):
    lanes = 2 * cells * cin
    both = [diagonals(own(tap), before(tap), cells, cout, cin) for tap in range(9)]
    ahead, behind = place([x for x, _ in both]), place([x for _, x in both])
    r, q = iotas((2 * cin, lanes))
    pick = jnp.where((q // cin % 2 == r // cin) & (q % cin == r % cin), 1.0, 0.0)
    r, q = iotas((max(cin, 8), lanes))
    every = jnp.where(q % cin == r, 1.0, 0.0)
    return [jnp.concatenate([exact_nt(pick, x), exact_nt(every, y)], axis=0) for x, y in zip(ahead, behind)]


def second_gradient_kernel(hh_ref, delta_ref, k2_ref, a_hbm, out_ref, t2b_ref, a_ref, sem):
    copy = pltpu.make_async_copy(a_hbm, a_ref, sem)
    copy.start()
    d2n = delta_ref.shape[0]
    delta = jnp.concatenate([delta_ref[d] for d in range(d2n)], axis=0)
    g = dot_tn(delta, second_layer_columns(hh_ref, d2n))
    none = [jnp.zeros((3 * C2, LH), f32)]
    _, q = iotas((C2, LH))
    (sums,) = width_sums(
        lambda tap: g[:, 2 * LH * tap : 2 * LH * tap + LH],
        lambda tap: jnp.where(q // C1 == W1 - 1, g[:C2, 2 * LH * tap + LH : 2 * LH * (tap + 1)], 0.0),
        W2,
        C2,
        C1,
        lambda taps: [jnp.concatenate(taps + none, axis=0)],
    )
    out_ref[...] = sums
    band_back(tiled(spread_back(k2_ref[...]), W2), LZ, C2, LH, C1, puts(t2b_ref, LZ))
    copy.wait()


def first_gradient_kernel(hh_ref, delta_ref, next_ref, t2b_ref, a_ref, two_ref, out_ref, dv_ref):
    d2n = delta_ref.shape[0]
    r, _ = iotas((ROWS, LZ))
    keep = r % HB != HB - 1
    none = jnp.zeros((HB, LZ), bf16)
    for d in range(d2n + 1):
        x = delta_ref[d] if d < d2n else next_ref[...]
        up = jnp.where(keep, pltpu.roll(x.astype(f32), ROWS - 1, 0), 0.0).astype(bf16)
        for v, y in enumerate((x, up)):
            dv_ref[d, v, :, :LZ] = y
            dv_ref[d, v, :, LZ:] = jnp.concatenate([y[HB:], none], axis=0)

    def pulled(first, kd, kh):
        v = 1 if kh == 0 else 0
        lhs = jnp.concatenate([dv_ref[d + first, v] for d in range(d2n)], axis=0)
        tap = 3 * kd + kh
        return lhs, t2b_ref[2 * LZ * tap : 2 * LZ * (tap + 1)]

    deltas, planes = [], []
    for p in range(2):
        heights = (1,) if p == 0 else (2, 0)
        for even in range(2):
            depths = ((0, 2), (1, 0)) if even else ((0, 1),)
            terms = [pulled(first, kd, kh) for first, kd in depths for kh in heights]
            back = dot(
                jnp.concatenate([lhs for lhs, _ in terms], axis=1),
                jnp.concatenate([rhs for _, rhs in terms], axis=0),
            )
            here = [(p, 2 * d + 1 + even) for d in range(d2n)]
            hidden = jnp.concatenate([hh_ref[j, 2 if p else 1] for _, j in here], axis=0)
            deltas.append((back * jnp.where(hidden.astype(f32) > 0, 1.0, SLOPE)).astype(bf16))
            planes += here
    g = dot_tn(jnp.concatenate(deltas, axis=0), first_layer_columns(a_ref, planes))
    before, after = [jnp.zeros((C2, LA), f32)], [jnp.zeros((128 - C2 - 3 * C1, LA), f32)]

    def place(taps):
        return [jnp.concatenate(before + taps[i : i + 3] + after, axis=0) for i in range(0, 9, 3)]

    _, q = iotas((C1, LA))
    sums = width_sums(
        lambda tap: g[:, LA * tap : LA * (tap + 1)],
        lambda tap: jnp.where(q // CIN % 8 == tap % 8, g[:C1, LA * (9 + tap // 8) : LA * (10 + tap // 8)], 0.0),
        W1,
        C1,
        CIN,
        place,
    )
    sums = jnp.concatenate(sums, axis=0)
    out_ref[: 3 * C1] = two_ref[:, :128]
    out_ref[3 * C1 : 6 * C1] = two_ref[:, 128:256]
    out_ref[6 * C1 :] = two_ref[:, 256:] + sums


def scale_kernel(factor, sum_ref, one_ref, two_ref):
    place = (2, 0, 1)
    for tap in range(9):
        for kw in range(3):
            r, q = 3 * C1 * (tap // 4) + C1 * place[kw], C2 * (tap % 4)
            two_ref[3 * tap + kw] = sum_ref[r : r + C1, q : q + C2] * factor
            r, q = 6 * C1 + C1 * (tap // 3) + CIN * place[kw], C2 + C1 * (tap % 3)
            one_ref[3 * tap + kw] = sum_ref[r : r + CIN, q : q + C1] * factor


def gather_kernel(
    vol_hbm, cot_hbm, k1_hbm, k2_hbm, vol_ref, out_ref, k1_ref, k2_ref, cot_ref, order_ref, sems
):
    d2n = vol_ref.shape[1] // 4
    copies = [
        pltpu.make_async_copy(x, y, sems.at[i])
        for i, (x, y) in enumerate(
            [(cot_hbm, cot_ref), (vol_hbm, vol_ref), (k1_hbm, k1_ref), (k2_hbm, k2_ref)]
        )
    ]
    for copy in copies:
        copy.start()
    channels, depth, cells = cot_ref.shape
    hl = cells // 32
    r, q = iotas((WIDE, WIDE))
    order_ref[...] = one_hot(q == (r % (BLOCKS * W2)) * C2 + r // (BLOCKS * W2))
    r, q = iotas((cells, hl * 128))
    moves = [one_hot((q // 128 == r // 32) & (q % 128 == i * 32 + r % 32)) for i in range(4)]
    copies[0].wait()
    parts = [
        dot(jnp.concatenate([cot_ref[first + i] for first in range(0, channels, 4)], axis=0), moves[i])
        for i in range(4)
    ]
    together = ((parts[0] + parts[1]) + (parts[2] + parts[3])).astype(bf16)
    groups = [together[i * depth : (i + 1) * depth] for i in range(channels // 4)]
    x = jnp.concatenate(
        [jnp.concatenate([g[:, h * 128 : (h + 1) * 128] for g in groups], axis=1) for h in range(hl)], axis=0
    )
    x = dot(x, order_ref[...]).astype(bf16)
    for device in range(out_ref.shape[0]):
        for h in range(hl):
            at = h * depth + device * d2n
            out_ref[device, h * d2n : (h + 1) * d2n] = x[at : at + d2n]
    for copy in copies[1:]:
        copy.wait()


def last_planes_kernel(vol_ref, low_ref):
    low_ref[...] = vol_ref[:, vol_ref.shape[1] - 3 :]


def scatter_kernel(d2n, got_ref, out_ref):
    channels, depth, cells = out_ref.shape
    hl = cells // 32
    count = got_ref.shape[0]
    r, q = iotas((count, count))
    row, plane = travel_order(q, depth, d2n, hl)
    got = dot(one_hot(r == row * depth + plane), got_ref[...]).astype(bf16)
    r, q = iotas((hl * 128, cells))
    moves = [one_hot((r // 128 == q // 32) & (r % 128 == i * 32 + q % 32)) for i in range(4)]
    groups = channels // 4
    for g in range(groups):
        x = jnp.concatenate(
            [got[(h * groups + g) * depth : (h * groups + g + 1) * depth] for h in range(hl)], axis=1
        )
        for i in range(4):
            out_ref[4 * g + i] = dot(x, moves[i]).astype(bf16)


def call(kernel, name, outs, *args, scratch=(), apart=(), apart_out=()):
    return pl.pallas_call(
        kernel,
        name=name,
        in_specs=[pl.BlockSpec(memory_space=pltpu.HBM if i in apart else pltpu.VMEM) for i in range(len(args))],
        out_specs=[
            pl.BlockSpec(memory_space=pltpu.HBM if i in apart_out else pltpu.VMEM) for i in range(len(outs))
        ],
        out_shape=[
            pltpu.HBM(shape, dtype) if i in apart_out else jax.ShapeDtypeStruct(shape, dtype)
            for i, (shape, dtype) in enumerate(outs)
        ],
        scratch_shapes=list(scratch),
        compiler_params=pltpu.CompilerParams(vmem_limit_bytes=32 << 20),
    )(*[pltpu.with_memory_space_constraint(x, pltpu.HBM) if i in apart else x for i, x in enumerate(args)])


def passed_along(block, distance):
    devices = range(lax.axis_size("space"))
    return lax.ppermute(block, "space", [(i - distance, i) for i in devices if i - distance in devices])


def with_partner(block, bit):
    count = lax.axis_size("dp") * lax.axis_size("space")
    return lax.ppermute(block, ("dp", "space"), [(i, i ^ bit) for i in range(count)])


def total_and_exchange(terms, rows):
    devices = lax.axis_size("space")
    here = lax.axis_index("space")
    count = rows.shape[0] // devices
    blocks = rows.reshape(devices, count, 128)
    half = terms.shape[0] // 2
    first, second = rows.shape[0] // 2, rows.shape[0] // 2 + half
    even = here % 2 == 0
    bit = 1
    while bit < devices:
        mine = (here // bit) % 2 == 0
        pairs = blocks.reshape(devices // (2 * bit), 2, bit, count, 128)
        kept = jnp.where(mine, pairs[:, 0], pairs[:, 1])
        sent = jnp.where(mine, pairs[:, 1], pairs[:, 0]).reshape(first, 128)
        high = lax.reduce_precision(terms, 8, 7)
        rest = lax.reduce_precision(terms - high, 8, 7)
        if bit == 1:
            stay = jnp.where(even, terms[:half], terms[half:])
            high, rest = (jnp.where(even, x[half:], x[:half]) for x in (high, rest))
        else:
            stay = high + rest
        got = with_partner(jnp.concatenate([sent, high.astype(bf16), rest.astype(bf16)], axis=0), bit)
        terms = stay + (got[first:second].astype(f32) + got[second:].astype(f32))
        came = got[:first].reshape(kept.shape)
        blocks = jnp.where(mine, jnp.stack([kept, came], 1), jnp.stack([came, kept], 1))
        bit *= 2
    while 2 * bit < devices * lax.axis_size("dp"):
        terms = terms + with_partner(terms, bit)
        bit *= 2
    beyond = [with_partner(terms, mask) for mask in (bit, 1, bit ^ 1)]
    return terms, beyond, blocks.reshape(rows.shape)


def rejoined(terms, beyond):
    mine, other = terms + beyond[0], beyond[1] + beyond[2]
    even = lax.axis_index("space") % 2 == 0
    return jnp.where(even, jnp.concatenate([mine, other], 0), jnp.concatenate([other, mine], 0))


def local(volumes, kernel_one, kernel_two, cotangent):
    _, _, planes, height, width = volumes.shape
    d1n, d2n = planes // 2, planes // 4
    _, _, depth, cells = cotangent.shape
    vol, cot = volumes[0], cotangent[0]
    devices = lax.axis_size("space")
    travelling = depth * (cells // 32) * (C2 // 4)

    k1 = kernel_one.transpose(2, 3, 4, 1, 0).reshape(27, CIN, C1)
    k2 = kernel_two.transpose(2, 3, 4, 1, 0).reshape(27 * C1, C2)
    vol, cot_rows, k1, k2 = call(
        gather_kernel,
        "gather",
        [(vol.shape, bf16), ((devices, depth // devices * (cells // 32), WIDE), bf16), (k1.shape, bf16), (k2.shape, bf16)],
        vol,
        cot,
        k1,
        k2,
        scratch=[
            pltpu.VMEM(cot.shape, bf16),
            pltpu.VMEM((WIDE, WIDE), bf16),
            pltpu.SemaphoreType.DMA((4,)),
        ],
        apart=(0, 1, 2, 3),
    )
    (low,) = call(last_planes_kernel, "last_planes", [((CIN, 3, height, width), bf16)], vol)
    low = passed_along(low, 1)
    cot_here = lax.all_to_all(cot_rows, "space", 0, 0, tiled=True)

    a, hh, send, slope = call(
        forward_kernel,
        "forward",
        [
            ((planes + 3, 5, ROWS + HB, LA), bf16),
            ((d1n + 1, 3, ROWS, LH), bf16),
            ((travelling, 128), bf16),
            ((d2n, ROWS, LZ), bf16),
        ],
        vol,
        low,
        k1,
        k2,
        scratch=[
            pltpu.VMEM((planes + 3, 5, ROWS + HB, LA), bf16),
            pltpu.VMEM((11 * LA, LH), bf16),
            pltpu.VMEM((9 * 2 * LH, LZ), bf16),
            pltpu.SemaphoreType.DMA,
        ],
        apart_out=(0,),
    )
    (delta,) = call(delta_kernel, "delta", [((d2n, ROWS, LZ), bf16)], cot_here, slope)
    delta_next = passed_along(delta[0], -1)
    term_two, t2b, a = call(
        second_gradient_kernel,
        "second_gradient",
        [((3 * C1, 384), f32), ((9 * 2 * LZ, LH), bf16), (a.shape, bf16)],
        hh,
        delta,
        k2,
        a,
        scratch=[pltpu.SemaphoreType.DMA],
        apart=(3,),
    )
    (terms,) = call(
        first_gradient_kernel,
        "first_gradient",
        [((9 * C1, 128), f32)],
        hh,
        delta,
        delta_next,
        t2b,
        a,
        term_two,
        scratch=[pltpu.VMEM((d2n + 1, 2, ROWS, 2 * LZ), bf16)],
    )
    terms, beyond, got = total_and_exchange(terms, send)
    (out,) = call(functools.partial(scatter_kernel, d2n), "scatter", [((C2, depth, cells), bf16)], got)
    terms = rejoined(terms, beyond)
    count = volumes.shape[0] * lax.axis_size("dp")
    factor = 1.0 / math.sqrt(count * depth * (height // 4) ** 2)
    one, two = call(
        functools.partial(scale_kernel, factor),
        "scale",
        [((27, CIN, C1), f32), ((27, C1, C2), f32)],
        terms,
    )
    return (
        out[None],
        one.reshape(3, 3, 3, CIN, C1).transpose(4, 3, 0, 1, 2),
        two.reshape(3, 3, 3, C1, C2).transpose(4, 3, 0, 1, 2),
    )


def solution(mesh):
    placed = (P("dp", None, "space", None, None), P(), P(), P("dp", None, None, "space"))
    return jax.shard_map(
        local,
        mesh=mesh,
        in_specs=placed,
        out_specs=(P("dp", None, None, "space"), P(), P()),
        check_vma=False,
    )
```

```python
import functools
import math

import jax
import jax.numpy as jnp
from jax import lax
from jax.experimental import pallas as pl
from jax.experimental.pallas import tpu as pltpu
from jax.sharding import PartitionSpec as P

f32 = jnp.float32
bf16 = jnp.bfloat16

SLOPE = 0.3
BLOCKS = 4
HB = 32
CIN, C1, C2 = 4, 16, 32
W0, W1, W2 = 32, 16, 8
ROWS = BLOCKS * HB
LA, LH, LZ = W0 * CIN, W1 * C1, W2 * C2
EDGE = LA // BLOCKS
WIDE = BLOCKS * LZ
TAPS = [(kd, kh) for kd in range(3) for kh in range(3)]
INPUT_ROWS = {(0, 0): 4, (0, 1): 0, (0, 2): 1, (1, 0): 1, (1, 1): 2, (1, 2): 3}


def dot(a, b):
    return jnp.dot(a, b, preferred_element_type=f32)


def dot_nt(a, b):
    return lax.dot_general(a, b, (((1,), (1,)), ((), ())), preferred_element_type=f32)


def dot_tn(a, b):
    return lax.dot_general(a, b, (((0,), (0,)), ((), ())), preferred_element_type=f32)


def exact_nt(a, b):
    a = a.astype(bf16)
    total = None
    for _ in range(3):
        part = b.astype(bf16)
        b = b - part.astype(f32)
        total = dot_nt(a, part) if total is None else total + dot_nt(a, part)
    return total


def iotas(shape):
    rows, lanes = shape
    return lax.broadcasted_iota(jnp.int32, (rows, 1), 0), lax.broadcasted_iota(jnp.int32, (1, lanes), 1)


def one_hot(mask):
    return jnp.where(mask, 1.0, 0.0).astype(bf16)


def width_order():
    r, q = iotas((CIN * 128, (CIN + 1) * 128))
    own = (q % CIN) * 128 + (q // LA) * W0 + (q // CIN) % W0
    edge = (q % CIN) * 128 + (q % LA) // EDGE * W0 - 1
    return one_hot(r == jnp.where(q < CIN * 128, own, jnp.where(q % LA < EDGE, -1, edge)))


def height_order():
    r, q = iotas((5 * HB, 4 * HB))
    return one_hot(q == 4 * (r % HB) + jnp.where(r // HB == 4, -1, r // HB))


def channel_order():
    r, q = iotas((WIDE, WIDE))
    cells = BLOCKS * W2
    return one_hot(r == (q % cells) * C2 + q // cells)


def arrange_planes(planes, count, put):
    x = jnp.concatenate([planes(c) for c in range(CIN)], axis=1)
    y = dot(x, width_order()).astype(bf16)
    order = height_order()
    for d in range(count):
        z = dot(order, y[d * 128 : (d + 1) * 128]).astype(bf16)
        for v in range(5):
            put(d, v, [z[v * HB : (v + 1) * HB, b * LA : (b + 1) * LA] for b in range(BLOCKS + 1)])


def with_before(x):
    return jnp.concatenate([x, jnp.concatenate([jnp.zeros_like(x[:HB]), x[:-HB]], axis=0)], axis=1)


def first_layer_columns(a_ref, planes, skipped=0):
    _, q = iotas((HB, LA))
    times = [one_hot(q // CIN % 8 == t) for t in range(8)]
    blocks = [one_hot(q // EDGE == b) for b in range(BLOCKS)]
    cols = [[] for _ in range(11)]
    for p, j in planes:
        x = [a_ref[2 * j + kd - skipped, INPUT_ROWS[p, kh]] for kd, kh in TAPS]
        edges = [y[ROWS:] for y in x]
        eight = edges[0] * times[0]
        for t in range(1, 8):
            eight = eight + edges[t] * times[t]
        x = [y[:ROWS] for y in x]
        for y in (eight, edges[8] * times[0]):
            x.append(jnp.concatenate([y * m for m in blocks], axis=0))
        for col, y in zip(cols, x):
            col.append(y)
    return jnp.concatenate([jnp.concatenate(col, axis=0) for col in cols], axis=1)


def band(taps, rows, cin, cols, cout, put):
    r, q = iotas((rows, cols))
    w, o = r // cin, q // cout
    rel = w - 2 * o + 1
    last = (w == rows // cin - 1) & (o == 0)
    for tap in range(9):
        e = [taps(3 * tap + kw) for kw in range(3)]
        own = jnp.where(rel == 0, e[0], jnp.where(rel == 1, e[1], jnp.where(rel == 2, e[2], 0.0)))
        put(tap, own.astype(bf16), jnp.where(last, e[0], 0.0).astype(bf16))


def band_back(taps, rows, cout, cols, cin, put):
    r, q = iotas((rows, cols))
    w, o = q // cin, r // cout
    rel = w - 2 * o + 1
    last = (w == cols // cin - 1) & (o == 0)
    for tap in range(9):
        e = [taps(3 * tap + kw) for kw in range(3)]
        own = jnp.where(rel == 0, e[0], jnp.where(rel == 1, e[1], jnp.where(rel == 2, e[2], 0.0)))
        put(tap, own.astype(bf16), jnp.where(last, e[0], 0.0).astype(bf16))


def spread(k, cols):
    c, q = iotas((k.shape[1], cols))
    return dot(k, one_hot(q % k.shape[1] == c))


def spread_back(k2):
    r, q = iotas((C2, C2))
    flipped = dot_nt(one_hot(r == q), k2).astype(bf16)
    flipped = jnp.concatenate([flipped, jnp.zeros((C2, 512 - 27 * C1), bf16)], axis=1)
    stacked = jnp.concatenate([flipped[:, 128 * i : 128 * (i + 1)] for i in range(4)], axis=0)
    r, q = iotas((128, LH))
    parts = [dot(stacked, one_hot((r // C1 == g) & (q % C1 == r % C1))) for g in range(8)]
    return lambda t: parts[t % 8][C2 * (t // 8) : C2 * (t // 8 + 1)]


def shifted_down(x, keep):
    return jnp.where(keep, pltpu.roll(x.astype(f32), 1, 0), 0.0).astype(bf16)


def travel_order(r, depth, d2n, hl):
    groups = hl * C2 // 4
    return (r // d2n) % groups, r // (groups * d2n) * d2n + r % d2n


def by_height(r, d2n):
    group, plane, h2 = r // (d2n * HB), (r // HB) % d2n, r % HB
    return (h2 * (C2 // 4) + group) * d2n + plane


def puts(ref, half):
    def put(tap, own, other):
        ref[2 * half * tap : 2 * half * tap + half] = own
        ref[2 * half * tap + half : 2 * half * (tap + 1)] = other

    return put


def tiled(each, times):
    return lambda t: jnp.concatenate([each(t)] * times, axis=0)


def forward_kernel(
    vol_ref, low_ref, k1_ref, k2_ref, a_hbm, hh_ref, send_ref, slope_ref, a_ref, t1_ref, t2_ref, sem
):
    count = vol_ref.shape[1]
    planes = hh_ref.shape[0]
    d2n = slope_ref.shape[0]
    copy = pltpu.make_async_copy(a_ref.at[2:], a_hbm, sem)

    def put_from(first):
        def put(d, v, blocks):
            for b, x in enumerate(blocks):
                a_ref[first + d, v, b * HB : (b + 1) * HB] = x

        return put

    k1 = jnp.concatenate([k1_ref[t].astype(f32) for t in range(27) for _ in range(16 // CIN)], axis=0)
    k1 = spread(k1.astype(bf16), LH)
    def put_own(tap, own, _):
        t1_ref[LA * tap : LA * (tap + 1)] = own

    band(tiled(lambda t: k1[16 * t : 16 * (t + 1)], LA // 16), LA, CIN, LH, C1, put_own)
    _, q = iotas((LA, LH))
    for i, taps in enumerate((range(8), [8] * 8)):
        edge = jnp.concatenate([k1[48 * t : 48 * t + CIN] for _ in range(BLOCKS) for t in taps], axis=0)
        t1_ref[LA * (9 + i) : LA * (10 + i)] = jnp.where(q < C1, edge, 0.0).astype(bf16)
    k2 = spread(k2_ref[...], LZ)
    band(tiled(lambda t: k2[C1 * t : C1 * (t + 1)], W1), LH, C1, LZ, C2, puts(t2_ref, LH))
    arrange_planes(lambda c: low_ref[c].reshape(3 * 128, 128), 3, put_from(0))
    arrange_planes(lambda c: vol_ref[c].reshape(count * 128, 128), count, put_from(3))
    copy.start()

    r, _ = iotas((planes * ROWS, LH))
    keep = r % HB != 0
    for p in range(2):
        linear = dot(first_layer_columns(a_ref, [(p, j) for j in range(planes)]), t1_ref[...])
        hidden = jnp.where(linear > 0, linear, SLOPE * linear).astype(bf16)
        variants = [(1, hidden)] if p == 0 else [(2, hidden), (0, shifted_down(hidden, keep))]
        for v, x in variants:
            for j in range(planes):
                hh_ref[j, v] = x[j * ROWS : (j + 1) * ROWS]

    linear = dot(second_layer_columns(hh_ref, d2n), t2_ref[...])
    out = jnp.where(linear > 0, linear, SLOPE * linear).astype(bf16)
    positive = jnp.where(linear > 0, 1.0, 0.0).astype(bf16)
    for d in range(d2n):
        slope_ref[d] = positive[d * ROWS : (d + 1) * ROWS]
    wide = jnp.concatenate(
        [
            jnp.concatenate([out[d * ROWS + b * HB : d * ROWS + (b + 1) * HB] for b in range(BLOCKS)], axis=1)
            for d in range(d2n)
        ],
        axis=0,
    )
    groups = C2 // 4
    by_channel = dot(wide, channel_order()).astype(bf16)
    stacked = jnp.concatenate([by_channel[:, 128 * g : 128 * (g + 1)] for g in range(groups)], axis=0)
    r, q = iotas((stacked.shape[0], stacked.shape[0]))
    send_ref[...] = dot(one_hot(r == by_height(q, d2n)), stacked).astype(bf16)
    copy.wait()


def second_layer_columns(hh_ref, d2n):
    cols = [jnp.concatenate([with_before(hh_ref[2 * d + kd, kh]) for d in range(d2n)], axis=0) for kd, kh in TAPS]
    return jnp.concatenate(cols, axis=1)


def delta_kernel(cot_ref, slope_ref, delta_ref):
    d2n = delta_ref.shape[0]
    devices, lines, _ = cot_ref.shape
    hl = lines // d2n
    r, q = iotas((d2n * HB, devices * lines))
    plane, h2 = r // HB, r % HB
    order = one_hot(q == h2 // hl * lines + h2 % hl * d2n + plane)
    got = dot(order, jnp.concatenate([cot_ref[i] for i in range(devices)], axis=0))
    for d in range(d2n):
        for b in range(BLOCKS):
            c = got[d * HB : (d + 1) * HB, b * LZ : (b + 1) * LZ]
            slope = jnp.where(slope_ref[d, b * HB : (b + 1) * HB].astype(f32) > 0, 1.0, SLOPE)
            delta_ref[d, b * HB : (b + 1) * HB] = (c * slope).astype(bf16)


def diagonals(x, before, cells, cout, cin):
    lanes = 2 * cells * cin
    _, q = iotas((cout, lanes))
    w = q // cin
    ahead = jnp.zeros((cout, lanes), f32)
    behind = jnp.zeros((cout, lanes), f32)
    for o in range(cells):
        y = x[o * cout : (o + 1) * cout]
        ahead = jnp.where(w // 2 == o, y, ahead)
        if o:
            behind = jnp.where(w == 2 * o - 1, y, behind)
    return ahead, behind + before


def width_sums(own, before, cells, cout, cin, place):
    lanes = 2 * cells * cin
    both = [diagonals(own(tap), before(tap), cells, cout, cin) for tap in range(9)]
    ahead, behind = place([x for x, _ in both]), place([x for _, x in both])
    r, q = iotas((2 * cin, lanes))
    pick = jnp.where((q // cin % 2 == r // cin) & (q % cin == r % cin), 1.0, 0.0)
    r, q = iotas((max(cin, 8), lanes))
    every = jnp.where(q % cin == r, 1.0, 0.0)
    return [jnp.concatenate([exact_nt(pick, x), exact_nt(every, y)], axis=0) for x, y in zip(ahead, behind)]


def second_gradient_kernel(hh_ref, delta_ref, k2_ref, a_hbm, out_ref, t2b_ref, a_ref, sem):
    copy = pltpu.make_async_copy(a_hbm, a_ref, sem)
    copy.start()
    d2n = delta_ref.shape[0]
    delta = jnp.concatenate([delta_ref[d] for d in range(d2n)], axis=0)
    g = dot_tn(delta, second_layer_columns(hh_ref, d2n))
    none = [jnp.zeros((3 * C2, LH), f32)]
    _, q = iotas((C2, LH))
    (sums,) = width_sums(
        lambda tap: g[:, 2 * LH * tap : 2 * LH * tap + LH],
        lambda tap: jnp.where(q // C1 == W1 - 1, g[:C2, 2 * LH * tap + LH : 2 * LH * (tap + 1)], 0.0),
        W2,
        C2,
        C1,
        lambda taps: [jnp.concatenate(taps + none, axis=0)],
    )
    out_ref[...] = sums
    band_back(tiled(spread_back(k2_ref[...]), W2), LZ, C2, LH, C1, puts(t2b_ref, LZ))
    copy.wait()


def first_gradient_kernel(hh_ref, delta_ref, next_ref, t2b_ref, a_ref, two_ref, out_ref, dv_ref):
    d2n = delta_ref.shape[0]
    r, _ = iotas((ROWS, LZ))
    keep = r % HB != HB - 1
    none = jnp.zeros((HB, LZ), bf16)
    for d in range(d2n + 1):
        x = delta_ref[d] if d < d2n else next_ref[...]
        up = jnp.where(keep, pltpu.roll(x.astype(f32), ROWS - 1, 0), 0.0).astype(bf16)
        for v, y in enumerate((x, up)):
            dv_ref[d, v, :, :LZ] = y
            dv_ref[d, v, :, LZ:] = jnp.concatenate([y[HB:], none], axis=0)

    def pulled(first, kd, kh):
        v = 1 if kh == 0 else 0
        lhs = jnp.concatenate([dv_ref[d + first, v] for d in range(d2n)], axis=0)
        tap = 3 * kd + kh
        return lhs, t2b_ref[2 * LZ * tap : 2 * LZ * (tap + 1)]

    deltas, planes = [], []
    for p in range(2):
        heights = (1,) if p == 0 else (2, 0)
        for even in range(2):
            depths = ((0, 2), (1, 0)) if even else ((0, 1),)
            terms = [pulled(first, kd, kh) for first, kd in depths for kh in heights]
            back = dot(
                jnp.concatenate([lhs for lhs, _ in terms], axis=1),
                jnp.concatenate([rhs for _, rhs in terms], axis=0),
            )
            here = [(p, 2 * d + 1 + even) for d in range(d2n)]
            hidden = jnp.concatenate([hh_ref[j, 2 if p else 1] for _, j in here], axis=0)
            deltas.append((back * jnp.where(hidden.astype(f32) > 0, 1.0, SLOPE)).astype(bf16))
            planes += here
    g = dot_tn(jnp.concatenate(deltas, axis=0), first_layer_columns(a_ref, planes, 2))
    before, after = [jnp.zeros((C2, LA), f32)], [jnp.zeros((128 - C2 - 3 * C1, LA), f32)]

    def place(taps):
        return [jnp.concatenate(before + taps[i : i + 3] + after, axis=0) for i in range(0, 9, 3)]

    _, q = iotas((C1, LA))
    sums = width_sums(
        lambda tap: g[:, LA * tap : LA * (tap + 1)],
        lambda tap: jnp.where(q // CIN % 8 == tap % 8, g[:C1, LA * (9 + tap // 8) : LA * (10 + tap // 8)], 0.0),
        W1,
        C1,
        CIN,
        place,
    )
    sums = jnp.concatenate(sums, axis=0)
    out_ref[: 3 * C1] = two_ref[:, :128]
    out_ref[3 * C1 : 6 * C1] = two_ref[:, 128:256]
    out_ref[6 * C1 :] = two_ref[:, 256:] + sums


def scale_kernel(factor, sum_ref, one_ref, two_ref):
    place = (2, 0, 1)
    for tap in range(9):
        for kw in range(3):
            r, q = 3 * C1 * (tap // 4) + C1 * place[kw], C2 * (tap % 4)
            two_ref[3 * tap + kw] = sum_ref[r : r + C1, q : q + C2] * factor
            r, q = 6 * C1 + C1 * (tap // 3) + CIN * place[kw], C2 + C1 * (tap % 3)
            one_ref[3 * tap + kw] = sum_ref[r : r + CIN, q : q + C1] * factor


def gather_kernel(
    vol_hbm, cot_hbm, k1_hbm, k2_hbm, vol_ref, out_ref, k1_ref, k2_ref, cot_ref, order_ref, sems
):
    d2n = vol_ref.shape[1] // 4
    copies = [
        pltpu.make_async_copy(x, y, sems.at[i])
        for i, (x, y) in enumerate(
            [(cot_hbm, cot_ref), (vol_hbm, vol_ref), (k1_hbm, k1_ref), (k2_hbm, k2_ref)]
        )
    ]
    for copy in copies:
        copy.start()
    channels, depth, cells = cot_ref.shape
    hl = cells // 32
    r, q = iotas((WIDE, WIDE))
    order_ref[...] = one_hot(q == (r % (BLOCKS * W2)) * C2 + r // (BLOCKS * W2))
    r, q = iotas((cells, hl * 128))
    moves = [one_hot((q // 128 == r // 32) & (q % 128 == i * 32 + r % 32)) for i in range(4)]
    copies[0].wait()
    parts = [
        dot(jnp.concatenate([cot_ref[first + i] for first in range(0, channels, 4)], axis=0), moves[i])
        for i in range(4)
    ]
    together = ((parts[0] + parts[1]) + (parts[2] + parts[3])).astype(bf16)
    groups = [together[i * depth : (i + 1) * depth] for i in range(channels // 4)]
    x = jnp.concatenate(
        [jnp.concatenate([g[:, h * 128 : (h + 1) * 128] for g in groups], axis=1) for h in range(hl)], axis=0
    )
    x = dot(x, order_ref[...]).astype(bf16)
    for device in range(out_ref.shape[0]):
        for h in range(hl):
            at = h * depth + device * d2n
            out_ref[device, h * d2n : (h + 1) * d2n] = x[at : at + d2n]
    for copy in copies[1:]:
        copy.wait()


def last_planes_kernel(vol_ref, low_ref):
    low_ref[...] = vol_ref[:, vol_ref.shape[1] - 3 :]


def scatter_kernel(d2n, got_ref, out_ref):
    channels, depth, cells = out_ref.shape
    hl = cells // 32
    count = got_ref.shape[0]
    r, q = iotas((count, count))
    row, plane = travel_order(q, depth, d2n, hl)
    got = dot(one_hot(r == row * depth + plane), got_ref[...]).astype(bf16)
    r, q = iotas((hl * 128, cells))
    moves = [one_hot((r // 128 == q // 32) & (r % 128 == i * 32 + q % 32)) for i in range(4)]
    groups = channels // 4
    for g in range(groups):
        x = jnp.concatenate(
            [got[(h * groups + g) * depth : (h * groups + g + 1) * depth] for h in range(hl)], axis=1
        )
        for i in range(4):
            out_ref[4 * g + i] = dot(x, moves[i]).astype(bf16)


def call(kernel, name, outs, *args, scratch=(), apart=(), apart_out=()):
    return pl.pallas_call(
        kernel,
        name=name,
        in_specs=[pl.BlockSpec(memory_space=pltpu.HBM if i in apart else pltpu.VMEM) for i in range(len(args))],
        out_specs=[
            pl.BlockSpec(memory_space=pltpu.HBM if i in apart_out else pltpu.VMEM) for i in range(len(outs))
        ],
        out_shape=[
            pltpu.HBM(shape, dtype) if i in apart_out else jax.ShapeDtypeStruct(shape, dtype)
            for i, (shape, dtype) in enumerate(outs)
        ],
        scratch_shapes=list(scratch),
        compiler_params=pltpu.CompilerParams(vmem_limit_bytes=32 << 20),
    )(*[pltpu.with_memory_space_constraint(x, pltpu.HBM) if i in apart else x for i, x in enumerate(args)])


def passed_along(block, distance):
    devices = range(lax.axis_size("space"))
    return lax.ppermute(block, "space", [(i - distance, i) for i in devices if i - distance in devices])


def with_partner(block, bit):
    count = lax.axis_size("dp") * lax.axis_size("space")
    return lax.ppermute(block, ("dp", "space"), [(i, i ^ bit) for i in range(count)])


def total_and_exchange(terms, rows):
    devices = lax.axis_size("space")
    here = lax.axis_index("space")
    count = rows.shape[0] // devices
    blocks = rows.reshape(devices, count, 128)
    half = terms.shape[0] // 2
    first, second = rows.shape[0] // 2, rows.shape[0] // 2 + half
    even = here % 2 == 0
    bit = 1
    while bit < devices:
        mine = (here // bit) % 2 == 0
        pairs = blocks.reshape(devices // (2 * bit), 2, bit, count, 128)
        kept = jnp.where(mine, pairs[:, 0], pairs[:, 1])
        sent = jnp.where(mine, pairs[:, 1], pairs[:, 0]).reshape(first, 128)
        high = lax.reduce_precision(terms, 8, 7)
        rest = lax.reduce_precision(terms - high, 8, 7)
        if bit == 1:
            stay = jnp.where(even, terms[:half], terms[half:])
            high, rest = (jnp.where(even, x[half:], x[:half]) for x in (high, rest))
        else:
            stay = high + rest
        got = with_partner(jnp.concatenate([sent, high.astype(bf16), rest.astype(bf16)], axis=0), bit)
        terms = stay + (got[first:second].astype(f32) + got[second:].astype(f32))
        came = got[:first].reshape(kept.shape)
        blocks = jnp.where(mine, jnp.stack([kept, came], 1), jnp.stack([came, kept], 1))
        bit *= 2
    while 2 * bit < devices * lax.axis_size("dp"):
        terms = terms + with_partner(terms, bit)
        bit *= 2
    beyond = [with_partner(terms, mask) for mask in (bit, 1, bit ^ 1)]
    return terms, beyond, blocks.reshape(rows.shape)


def rejoined(terms, beyond):
    mine, other = terms + beyond[0], beyond[1] + beyond[2]
    even = lax.axis_index("space") % 2 == 0
    return jnp.where(even, jnp.concatenate([mine, other], 0), jnp.concatenate([other, mine], 0))


def local(volumes, kernel_one, kernel_two, cotangent):
    _, _, planes, height, width = volumes.shape
    d1n, d2n = planes // 2, planes // 4
    _, _, depth, cells = cotangent.shape
    vol, cot = volumes[0], cotangent[0]
    devices = lax.axis_size("space")
    travelling = depth * (cells // 32) * (C2 // 4)

    k1 = kernel_one.transpose(2, 3, 4, 1, 0).reshape(27, CIN, C1)
    k2 = kernel_two.transpose(2, 3, 4, 1, 0).reshape(27 * C1, C2)
    vol, cot_rows, k1, k2 = call(
        gather_kernel,
        "gather",
        [(vol.shape, bf16), ((devices, depth // devices * (cells // 32), WIDE), bf16), (k1.shape, bf16), (k2.shape, bf16)],
        vol,
        cot,
        k1,
        k2,
        scratch=[
            pltpu.VMEM(cot.shape, bf16),
            pltpu.VMEM((WIDE, WIDE), bf16),
            pltpu.SemaphoreType.DMA((4,)),
        ],
        apart=(0, 1, 2, 3),
    )
    (low,) = call(last_planes_kernel, "last_planes", [((CIN, 3, height, width), bf16)], vol)
    low = passed_along(low, 1)
    cot_here = lax.all_to_all(cot_rows, "space", 0, 0, tiled=True)

    a, hh, send, slope = call(
        forward_kernel,
        "forward",
        [
            ((planes + 1, 5, ROWS + HB, LA), bf16),
            ((d1n + 1, 3, ROWS, LH), bf16),
            ((travelling, 128), bf16),
            ((d2n, ROWS, LZ), bf16),
        ],
        vol,
        low,
        k1,
        k2,
        scratch=[
            pltpu.VMEM((planes + 3, 5, ROWS + HB, LA), bf16),
            pltpu.VMEM((11 * LA, LH), bf16),
            pltpu.VMEM((9 * 2 * LH, LZ), bf16),
            pltpu.SemaphoreType.DMA,
        ],
        apart_out=(0,),
    )
    (delta,) = call(delta_kernel, "delta", [((d2n, ROWS, LZ), bf16)], cot_here, slope)
    delta_next = passed_along(delta[0], -1)
    term_two, t2b, a = call(
        second_gradient_kernel,
        "second_gradient",
        [((3 * C1, 384), f32), ((9 * 2 * LZ, LH), bf16), (a.shape, bf16)],
        hh,
        delta,
        k2,
        a,
        scratch=[pltpu.SemaphoreType.DMA],
        apart=(3,),
    )
    (terms,) = call(
        first_gradient_kernel,
        "first_gradient",
        [((9 * C1, 128), f32)],
        hh,
        delta,
        delta_next,
        t2b,
        a,
        term_two,
        scratch=[pltpu.VMEM((d2n + 1, 2, ROWS, 2 * LZ), bf16)],
    )
    terms, beyond, got = total_and_exchange(terms, send)
    (out,) = call(functools.partial(scatter_kernel, d2n), "scatter", [((C2, depth, cells), bf16)], got)
    terms = rejoined(terms, beyond)
    count = volumes.shape[0] * lax.axis_size("dp")
    factor = 1.0 / math.sqrt(count * depth * (height // 4) ** 2)
    one, two = call(
        functools.partial(scale_kernel, factor),
        "scale",
        [((27, CIN, C1), f32), ((27, C1, C2), f32)],
        terms,
    )
    return (
        out[None],
        one.reshape(3, 3, 3, CIN, C1).transpose(4, 3, 0, 1, 2),
        two.reshape(3, 3, 3, C1, C2).transpose(4, 3, 0, 1, 2),
    )


def solution(mesh):
    placed = (P("dp", None, "space", None, None), P(), P(), P("dp", None, None, "space"))
    return jax.shard_map(
        local,
        mesh=mesh,
        in_specs=placed,
        out_specs=(P("dp", None, None, "space"), P(), P()),
        check_vma=False,
    )
```

```python
import functools
import math

import jax
import jax.numpy as jnp
from jax import lax
from jax.experimental import pallas as pl
from jax.experimental.pallas import tpu as pltpu
from jax.sharding import PartitionSpec as P

f32 = jnp.float32
bf16 = jnp.bfloat16

SLOPE = 0.3
BLOCKS = 4
HB = 32
CIN, C1, C2 = 4, 16, 32
W0, W1, W2 = 32, 16, 8
ROWS = BLOCKS * HB
LA, LH, LZ = W0 * CIN, W1 * C1, W2 * C2
EDGE = LA // BLOCKS
WIDE = BLOCKS * LZ
TAPS = [(kd, kh) for kd in range(3) for kh in range(3)]
INPUT_ROWS = {(0, 0): 4, (0, 1): 0, (0, 2): 1, (1, 0): 1, (1, 1): 2, (1, 2): 3}


def dot(a, b):
    return jnp.dot(a, b, preferred_element_type=f32)


def dot_nt(a, b):
    return lax.dot_general(a, b, (((1,), (1,)), ((), ())), preferred_element_type=f32)


def dot_tn(a, b):
    return lax.dot_general(a, b, (((0,), (0,)), ((), ())), preferred_element_type=f32)


def exact_nt(a, b):
    a = a.astype(bf16)
    total = None
    for _ in range(2):
        part = b.astype(bf16)
        b = b - part.astype(f32)
        total = dot_nt(a, part) if total is None else total + dot_nt(a, part)
    return total


def iotas(shape):
    rows, lanes = shape
    return lax.broadcasted_iota(jnp.int32, (rows, 1), 0), lax.broadcasted_iota(jnp.int32, (1, lanes), 1)


def one_hot(mask):
    return jnp.where(mask, 1.0, 0.0).astype(bf16)


def width_order():
    r, q = iotas((CIN * 128, (CIN + 1) * 128))
    own = (q % CIN) * 128 + (q // LA) * W0 + (q // CIN) % W0
    edge = (q % CIN) * 128 + (q % LA) // EDGE * W0 - 1
    return one_hot(r == jnp.where(q < CIN * 128, own, jnp.where(q % LA < EDGE, -1, edge)))


def height_order():
    r, q = iotas((5 * HB, 4 * HB))
    return one_hot(q == 4 * (r % HB) + jnp.where(r // HB == 4, -1, r // HB))


def channel_order():
    r, q = iotas((WIDE, WIDE))
    cells = BLOCKS * W2
    return one_hot(r == (q % cells) * C2 + q // cells)


def arrange_planes(planes, count, put):
    x = jnp.concatenate([planes(c) for c in range(CIN)], axis=1)
    y = dot(x, width_order()).astype(bf16)
    order = height_order()
    for d in range(count):
        z = dot(order, y[d * 128 : (d + 1) * 128]).astype(bf16)
        for v in range(5):
            put(d, v, [z[v * HB : (v + 1) * HB, b * LA : (b + 1) * LA] for b in range(BLOCKS + 1)])


def with_before(x):
    return jnp.concatenate([x, jnp.concatenate([jnp.zeros_like(x[:HB]), x[:-HB]], axis=0)], axis=1)


def first_layer_columns(a_ref, planes):
    _, q = iotas((HB, LA))
    times = [one_hot(q // CIN % 8 == t) for t in range(8)]
    blocks = [one_hot(q // EDGE == b) for b in range(BLOCKS)]
    cols = [[] for _ in range(11)]
    for p, j in planes:
        x = [a_ref[2 * j + kd, INPUT_ROWS[p, kh]] for kd, kh in TAPS]
        edges = [y[ROWS:] for y in x]
        eight = edges[0] * times[0]
        for t in range(1, 8):
            eight = eight + edges[t] * times[t]
        x = [y[:ROWS] for y in x]
        for y in (eight, edges[8] * times[0]):
            x.append(jnp.concatenate([y * m for m in blocks], axis=0))
        for col, y in zip(cols, x):
            col.append(y)
    return jnp.concatenate([jnp.concatenate(col, axis=0) for col in cols], axis=1)


def band(taps, rows, cin, cols, cout, put):
    r, q = iotas((rows, cols))
    w, o = r // cin, q // cout
    rel = w - 2 * o + 1
    last = (w == rows // cin - 1) & (o == 0)
    for tap in range(9):
        e = [taps(3 * tap + kw) for kw in range(3)]
        own = jnp.where(rel == 0, e[0], jnp.where(rel == 1, e[1], jnp.where(rel == 2, e[2], 0.0)))
        put(tap, own.astype(bf16), jnp.where(last, e[0], 0.0).astype(bf16))


def band_back(taps, rows, cout, cols, cin, put):
    r, q = iotas((rows, cols))
    w, o = q // cin, r // cout
    rel = w - 2 * o + 1
    last = (w == cols // cin - 1) & (o == 0)
    for tap in range(9):
        e = [taps(3 * tap + kw) for kw in range(3)]
        own = jnp.where(rel == 0, e[0], jnp.where(rel == 1, e[1], jnp.where(rel == 2, e[2], 0.0)))
        put(tap, own.astype(bf16), jnp.where(last, e[0], 0.0).astype(bf16))


def spread(k, cols):
    c, q = iotas((k.shape[1], cols))
    return dot(k, one_hot(q % k.shape[1] == c))


def spread_back(k2):
    r, q = iotas((C2, C2))
    flipped = dot_nt(one_hot(r == q), k2).astype(bf16)
    flipped = jnp.concatenate([flipped, jnp.zeros((C2, 512 - 27 * C1), bf16)], axis=1)
    stacked = jnp.concatenate([flipped[:, 128 * i : 128 * (i + 1)] for i in range(4)], axis=0)
    r, q = iotas((128, LH))
    parts = [dot(stacked, one_hot((r // C1 == g) & (q % C1 == r % C1))) for g in range(8)]
    return lambda t: parts[t % 8][C2 * (t // 8) : C2 * (t // 8 + 1)]


def shifted_down(x, keep):
    return jnp.where(keep, pltpu.roll(x.astype(f32), 1, 0), 0.0).astype(bf16)


def travel_order(r, depth, d2n, hl):
    groups = hl * C2 // 4
    return (r // d2n) % groups, r // (groups * d2n) * d2n + r % d2n


def by_height(r, d2n):
    group, plane, h2 = r // (d2n * HB), (r // HB) % d2n, r % HB
    return (h2 * (C2 // 4) + group) * d2n + plane


def puts(ref, half):
    def put(tap, own, other):
        ref[2 * half * tap : 2 * half * tap + half] = own
        ref[2 * half * tap + half : 2 * half * (tap + 1)] = other

    return put


def tiled(each, times):
    return lambda t: jnp.concatenate([each(t)] * times, axis=0)


def forward_kernel(
    vol_ref, low_ref, k1_ref, k2_ref, a_hbm, hh_ref, send_ref, slope_ref, a_ref, t1_ref, t2_ref, sem
):
    count = vol_ref.shape[1]
    planes = hh_ref.shape[0]
    d2n = slope_ref.shape[0]
    copy = pltpu.make_async_copy(a_ref, a_hbm, sem)

    def put_from(first):
        def put(d, v, blocks):
            for b, x in enumerate(blocks):
                a_ref[first + d, v, b * HB : (b + 1) * HB] = x

        return put

    k1 = jnp.concatenate([k1_ref[t].astype(f32) for t in range(27) for _ in range(16 // CIN)], axis=0)
    k1 = spread(k1.astype(bf16), LH)
    def put_own(tap, own, _):
        t1_ref[LA * tap : LA * (tap + 1)] = own

    band(tiled(lambda t: k1[16 * t : 16 * (t + 1)], LA // 16), LA, CIN, LH, C1, put_own)
    _, q = iotas((LA, LH))
    for i, taps in enumerate((range(8), [8] * 8)):
        edge = jnp.concatenate([k1[48 * t : 48 * t + CIN] for _ in range(BLOCKS) for t in taps], axis=0)
        t1_ref[LA * (9 + i) : LA * (10 + i)] = jnp.where(q < C1, edge, 0.0).astype(bf16)
    k2 = spread(k2_ref[...], LZ)
    band(tiled(lambda t: k2[C1 * t : C1 * (t + 1)], W1), LH, C1, LZ, C2, puts(t2_ref, LH))
    arrange_planes(lambda c: low_ref[c].reshape(3 * 128, 128), 3, put_from(0))
    arrange_planes(lambda c: vol_ref[c].reshape(count * 128, 128), count, put_from(3))
    copy.start()

    r, _ = iotas((planes * ROWS, LH))
    keep = r % HB != 0
    for p in range(2):
        linear = dot(first_layer_columns(a_ref, [(p, j) for j in range(planes)]), t1_ref[...])
        hidden = jnp.where(linear > 0, linear, SLOPE * linear).astype(bf16)
        variants = [(1, hidden)] if p == 0 else [(2, hidden), (0, shifted_down(hidden, keep))]
        for v, x in variants:
            for j in range(planes):
                hh_ref[j, v] = x[j * ROWS : (j + 1) * ROWS]

    linear = dot(second_layer_columns(hh_ref, d2n), t2_ref[...])
    out = jnp.where(linear > 0, linear, SLOPE * linear).astype(bf16)
    positive = jnp.where(linear > 0, 1.0, 0.0).astype(bf16)
    for d in range(d2n):
        slope_ref[d] = positive[d * ROWS : (d + 1) * ROWS]
    wide = jnp.concatenate(
        [
            jnp.concatenate([out[d * ROWS + b * HB : d * ROWS + (b + 1) * HB] for b in range(BLOCKS)], axis=1)
            for d in range(d2n)
        ],
        axis=0,
    )
    groups = C2 // 4
    by_channel = dot(wide, channel_order()).astype(bf16)
    stacked = jnp.concatenate([by_channel[:, 128 * g : 128 * (g + 1)] for g in range(groups)], axis=0)
    r, q = iotas((stacked.shape[0], stacked.shape[0]))
    send_ref[...] = dot(one_hot(r == by_height(q, d2n)), stacked).astype(bf16)
    copy.wait()


def second_layer_columns(hh_ref, d2n):
    cols = [jnp.concatenate([with_before(hh_ref[2 * d + kd, kh]) for d in range(d2n)], axis=0) for kd, kh in TAPS]
    return jnp.concatenate(cols, axis=1)


def delta_kernel(cot_ref, slope_ref, delta_ref):
    d2n = delta_ref.shape[0]
    devices, lines, _ = cot_ref.shape
    hl = lines // d2n
    r, q = iotas((d2n * HB, devices * lines))
    plane, h2 = r // HB, r % HB
    order = one_hot(q == h2 // hl * lines + h2 % hl * d2n + plane)
    got = dot(order, jnp.concatenate([cot_ref[i] for i in range(devices)], axis=0))
    for d in range(d2n):
        for b in range(BLOCKS):
            c = got[d * HB : (d + 1) * HB, b * LZ : (b + 1) * LZ]
            slope = jnp.where(slope_ref[d, b * HB : (b + 1) * HB].astype(f32) > 0, 1.0, SLOPE)
            delta_ref[d, b * HB : (b + 1) * HB] = (c * slope).astype(bf16)


def diagonals(x, before, cells, cout, cin):
    lanes = 2 * cells * cin
    _, q = iotas((cout, lanes))
    w = q // cin
    ahead = jnp.zeros((cout, lanes), f32)
    behind = jnp.zeros((cout, lanes), f32)
    for o in range(cells):
        y = x[o * cout : (o + 1) * cout]
        ahead = jnp.where(w // 2 == o, y, ahead)
        if o:
            behind = jnp.where(w == 2 * o - 1, y, behind)
    return ahead, behind + before


def width_sums(own, before, cells, cout, cin, place):
    lanes = 2 * cells * cin
    both = [diagonals(own(tap), before(tap), cells, cout, cin) for tap in range(9)]
    ahead, behind = place([x for x, _ in both]), place([x for _, x in both])
    r, q = iotas((2 * cin, lanes))
    pick = jnp.where((q // cin % 2 == r // cin) & (q % cin == r % cin), 1.0, 0.0)
    r, q = iotas((max(cin, 8), lanes))
    every = jnp.where(q % cin == r, 1.0, 0.0)
    return [jnp.concatenate([exact_nt(pick, x), exact_nt(every, y)], axis=0) for x, y in zip(ahead, behind)]


def second_gradient_kernel(hh_ref, delta_ref, k2_ref, a_hbm, out_ref, t2b_ref, a_ref, sem):
    copy = pltpu.make_async_copy(a_hbm, a_ref, sem)
    copy.start()
    d2n = delta_ref.shape[0]
    delta = jnp.concatenate([delta_ref[d] for d in range(d2n)], axis=0)
    g = dot_tn(delta, second_layer_columns(hh_ref, d2n))
    none = [jnp.zeros((3 * C2, LH), f32)]
    _, q = iotas((C2, LH))
    (sums,) = width_sums(
        lambda tap: g[:, 2 * LH * tap : 2 * LH * tap + LH],
        lambda tap: jnp.where(q // C1 == W1 - 1, g[:C2, 2 * LH * tap + LH : 2 * LH * (tap + 1)], 0.0),
        W2,
        C2,
        C1,
        lambda taps: [jnp.concatenate(taps + none, axis=0)],
    )
    out_ref[...] = sums
    band_back(tiled(spread_back(k2_ref[...]), W2), LZ, C2, LH, C1, puts(t2b_ref, LZ))
    copy.wait()


def first_gradient_kernel(hh_ref, delta_ref, next_ref, t2b_ref, a_ref, two_ref, out_ref, dv_ref):
    d2n = delta_ref.shape[0]
    r, _ = iotas((ROWS, LZ))
    keep = r % HB != HB - 1
    none = jnp.zeros((HB, LZ), bf16)
    for d in range(d2n + 1):
        x = delta_ref[d] if d < d2n else next_ref[...]
        up = jnp.where(keep, pltpu.roll(x.astype(f32), ROWS - 1, 0), 0.0).astype(bf16)
        for v, y in enumerate((x, up)):
            dv_ref[d, v, :, :LZ] = y
            dv_ref[d, v, :, LZ:] = jnp.concatenate([y[HB:], none], axis=0)

    def pulled(first, kd, kh):
        v = 1 if kh == 0 else 0
        lhs = jnp.concatenate([dv_ref[d + first, v] for d in range(d2n)], axis=0)
        tap = 3 * kd + kh
        return lhs, t2b_ref[2 * LZ * tap : 2 * LZ * (tap + 1)]

    deltas, planes = [], []
    for p in range(2):
        heights = (1,) if p == 0 else (2, 0)
        for even in range(2):
            depths = ((0, 2), (1, 0)) if even else ((0, 1),)
            terms = [pulled(first, kd, kh) for first, kd in depths for kh in heights]
            back = dot(
                jnp.concatenate([lhs for lhs, _ in terms], axis=1),
                jnp.concatenate([rhs for _, rhs in terms], axis=0),
            )
            here = [(p, 2 * d + 1 + even) for d in range(d2n)]
            hidden = jnp.concatenate([hh_ref[j, 2 if p else 1] for _, j in here], axis=0)
            deltas.append((back * jnp.where(hidden.astype(f32) > 0, 1.0, SLOPE)).astype(bf16))
            planes += here
    g = dot_tn(jnp.concatenate(deltas, axis=0), first_layer_columns(a_ref, planes))
    before, after = [jnp.zeros((C2, LA), f32)], [jnp.zeros((128 - C2 - 3 * C1, LA), f32)]

    def place(taps):
        return [jnp.concatenate(before + taps[i : i + 3] + after, axis=0) for i in range(0, 9, 3)]

    _, q = iotas((C1, LA))
    sums = width_sums(
        lambda tap: g[:, LA * tap : LA * (tap + 1)],
        lambda tap: jnp.where(q // CIN % 8 == tap % 8, g[:C1, LA * (9 + tap // 8) : LA * (10 + tap // 8)], 0.0),
        W1,
        C1,
        CIN,
        place,
    )
    sums = jnp.concatenate(sums, axis=0)
    out_ref[: 3 * C1] = two_ref[:, :128]
    out_ref[3 * C1 : 6 * C1] = two_ref[:, 128:256]
    out_ref[6 * C1 :] = two_ref[:, 256:] + sums


def scale_kernel(factor, sum_ref, one_ref, two_ref):
    place = (2, 0, 1)
    for tap in range(9):
        for kw in range(3):
            r, q = 3 * C1 * (tap // 4) + C1 * place[kw], C2 * (tap % 4)
            two_ref[3 * tap + kw] = sum_ref[r : r + C1, q : q + C2] * factor
            r, q = 6 * C1 + C1 * (tap // 3) + CIN * place[kw], C2 + C1 * (tap % 3)
            one_ref[3 * tap + kw] = sum_ref[r : r + CIN, q : q + C1] * factor


def gather_kernel(
    vol_hbm, cot_hbm, k1_hbm, k2_hbm, vol_ref, out_ref, k1_ref, k2_ref, cot_ref, order_ref, sems
):
    d2n = vol_ref.shape[1] // 4
    copies = [
        pltpu.make_async_copy(x, y, sems.at[i])
        for i, (x, y) in enumerate(
            [(cot_hbm, cot_ref), (vol_hbm, vol_ref), (k1_hbm, k1_ref), (k2_hbm, k2_ref)]
        )
    ]
    for copy in copies:
        copy.start()
    channels, depth, cells = cot_ref.shape
    hl = cells // 32
    r, q = iotas((WIDE, WIDE))
    order_ref[...] = one_hot(q == (r % (BLOCKS * W2)) * C2 + r // (BLOCKS * W2))
    r, q = iotas((cells, hl * 128))
    moves = [one_hot((q // 128 == r // 32) & (q % 128 == i * 32 + r % 32)) for i in range(4)]
    copies[0].wait()
    parts = [
        dot(jnp.concatenate([cot_ref[first + i] for first in range(0, channels, 4)], axis=0), moves[i])
        for i in range(4)
    ]
    together = ((parts[0] + parts[1]) + (parts[2] + parts[3])).astype(bf16)
    groups = [together[i * depth : (i + 1) * depth] for i in range(channels // 4)]
    x = jnp.concatenate(
        [jnp.concatenate([g[:, h * 128 : (h + 1) * 128] for g in groups], axis=1) for h in range(hl)], axis=0
    )
    x = dot(x, order_ref[...]).astype(bf16)
    for device in range(out_ref.shape[0]):
        for h in range(hl):
            at = h * depth + device * d2n
            out_ref[device, h * d2n : (h + 1) * d2n] = x[at : at + d2n]
    for copy in copies[1:]:
        copy.wait()


def last_planes_kernel(vol_ref, low_ref):
    low_ref[...] = vol_ref[:, vol_ref.shape[1] - 3 :]


def scatter_kernel(d2n, got_ref, out_ref):
    channels, depth, cells = out_ref.shape
    hl = cells // 32
    count = got_ref.shape[0]
    r, q = iotas((count, count))
    row, plane = travel_order(q, depth, d2n, hl)
    got = dot(one_hot(r == row * depth + plane), got_ref[...]).astype(bf16)
    r, q = iotas((hl * 128, cells))
    moves = [one_hot((r // 128 == q // 32) & (r % 128 == i * 32 + q % 32)) for i in range(4)]
    groups = channels // 4
    for g in range(groups):
        x = jnp.concatenate(
            [got[(h * groups + g) * depth : (h * groups + g + 1) * depth] for h in range(hl)], axis=1
        )
        for i in range(4):
            out_ref[4 * g + i] = dot(x, moves[i]).astype(bf16)


def call(kernel, name, outs, *args, scratch=(), apart=(), apart_out=()):
    return pl.pallas_call(
        kernel,
        name=name,
        in_specs=[pl.BlockSpec(memory_space=pltpu.HBM if i in apart else pltpu.VMEM) for i in range(len(args))],
        out_specs=[
            pl.BlockSpec(memory_space=pltpu.HBM if i in apart_out else pltpu.VMEM) for i in range(len(outs))
        ],
        out_shape=[
            pltpu.HBM(shape, dtype) if i in apart_out else jax.ShapeDtypeStruct(shape, dtype)
            for i, (shape, dtype) in enumerate(outs)
        ],
        scratch_shapes=list(scratch),
        compiler_params=pltpu.CompilerParams(vmem_limit_bytes=32 << 20),
    )(*[pltpu.with_memory_space_constraint(x, pltpu.HBM) if i in apart else x for i, x in enumerate(args)])


def passed_along(block, distance):
    devices = range(lax.axis_size("space"))
    return lax.ppermute(block, "space", [(i - distance, i) for i in devices if i - distance in devices])


def with_partner(block, bit):
    count = lax.axis_size("dp") * lax.axis_size("space")
    return lax.ppermute(block, ("dp", "space"), [(i, i ^ bit) for i in range(count)])


def total_and_exchange(terms, rows):
    devices = lax.axis_size("space")
    here = lax.axis_index("space")
    count = rows.shape[0] // devices
    blocks = rows.reshape(devices, count, 128)
    half = terms.shape[0] // 2
    first, second = rows.shape[0] // 2, rows.shape[0] // 2 + half
    even = here % 2 == 0
    bit = 1
    while bit < devices:
        mine = (here // bit) % 2 == 0
        pairs = blocks.reshape(devices // (2 * bit), 2, bit, count, 128)
        kept = jnp.where(mine, pairs[:, 0], pairs[:, 1])
        sent = jnp.where(mine, pairs[:, 1], pairs[:, 0]).reshape(first, 128)
        high = lax.reduce_precision(terms, 8, 7)
        rest = lax.reduce_precision(terms - high, 8, 7)
        if bit == 1:
            stay = jnp.where(even, terms[:half], terms[half:])
            high, rest = (jnp.where(even, x[half:], x[:half]) for x in (high, rest))
        else:
            stay = high + rest
        got = with_partner(jnp.concatenate([sent, high.astype(bf16), rest.astype(bf16)], axis=0), bit)
        terms = stay + (got[first:second].astype(f32) + got[second:].astype(f32))
        came = got[:first].reshape(kept.shape)
        blocks = jnp.where(mine, jnp.stack([kept, came], 1), jnp.stack([came, kept], 1))
        bit *= 2
    while 2 * bit < devices * lax.axis_size("dp"):
        terms = terms + with_partner(terms, bit)
        bit *= 2
    beyond = [with_partner(terms, mask) for mask in (bit, 1, bit ^ 1)]
    return terms, beyond, blocks.reshape(rows.shape)


def rejoined(terms, beyond):
    mine, other = terms + beyond[0], beyond[1] + beyond[2]
    even = lax.axis_index("space") % 2 == 0
    return jnp.where(even, jnp.concatenate([mine, other], 0), jnp.concatenate([other, mine], 0))


def local(volumes, kernel_one, kernel_two, cotangent):
    _, _, planes, height, width = volumes.shape
    d1n, d2n = planes // 2, planes // 4
    _, _, depth, cells = cotangent.shape
    vol, cot = volumes[0], cotangent[0]
    devices = lax.axis_size("space")
    travelling = depth * (cells // 32) * (C2 // 4)

    k1 = kernel_one.transpose(2, 3, 4, 1, 0).reshape(27, CIN, C1)
    k2 = kernel_two.transpose(2, 3, 4, 1, 0).reshape(27 * C1, C2)
    vol, cot_rows, k1, k2 = call(
        gather_kernel,
        "gather",
        [(vol.shape, bf16), ((devices, depth // devices * (cells // 32), WIDE), bf16), (k1.shape, bf16), (k2.shape, bf16)],
        vol,
        cot,
        k1,
        k2,
        scratch=[
            pltpu.VMEM(cot.shape, bf16),
            pltpu.VMEM((WIDE, WIDE), bf16),
            pltpu.SemaphoreType.DMA((4,)),
        ],
        apart=(0, 1, 2, 3),
    )
    (low,) = call(last_planes_kernel, "last_planes", [((CIN, 3, height, width), bf16)], vol)
    low = passed_along(low, 1)
    cot_here = lax.all_to_all(cot_rows, "space", 0, 0, tiled=True)

    a, hh, send, slope = call(
        forward_kernel,
        "forward",
        [
            ((planes + 3, 5, ROWS + HB, LA), bf16),
            ((d1n + 1, 3, ROWS, LH), bf16),
            ((travelling, 128), bf16),
            ((d2n, ROWS, LZ), bf16),
        ],
        vol,
        low,
        k1,
        k2,
        scratch=[
            pltpu.VMEM((planes + 3, 5, ROWS + HB, LA), bf16),
            pltpu.VMEM((11 * LA, LH), bf16),
            pltpu.VMEM((9 * 2 * LH, LZ), bf16),
            pltpu.SemaphoreType.DMA,
        ],
        apart_out=(0,),
    )
    (delta,) = call(delta_kernel, "delta", [((d2n, ROWS, LZ), bf16)], cot_here, slope)
    delta_next = passed_along(delta[0], -1)
    term_two, t2b, a = call(
        second_gradient_kernel,
        "second_gradient",
        [((3 * C1, 384), f32), ((9 * 2 * LZ, LH), bf16), (a.shape, bf16)],
        hh,
        delta,
        k2,
        a,
        scratch=[pltpu.SemaphoreType.DMA],
        apart=(3,),
    )
    (terms,) = call(
        first_gradient_kernel,
        "first_gradient",
        [((9 * C1, 128), f32)],
        hh,
        delta,
        delta_next,
        t2b,
        a,
        term_two,
        scratch=[pltpu.VMEM((d2n + 1, 2, ROWS, 2 * LZ), bf16)],
    )
    terms, beyond, got = total_and_exchange(terms, send)
    (out,) = call(functools.partial(scatter_kernel, d2n), "scatter", [((C2, depth, cells), bf16)], got)
    terms = rejoined(terms, beyond)
    count = volumes.shape[0] * lax.axis_size("dp")
    factor = 1.0 / math.sqrt(count * depth * (height // 4) ** 2)
    one, two = call(
        functools.partial(scale_kernel, factor),
        "scale",
        [((27, CIN, C1), f32), ((27, C1, C2), f32)],
        terms,
    )
    return (
        out[None],
        one.reshape(3, 3, 3, CIN, C1).transpose(4, 3, 0, 1, 2),
        two.reshape(3, 3, 3, C1, C2).transpose(4, 3, 0, 1, 2),
    )


def solution(mesh):
    placed = (P("dp", None, "space", None, None), P(), P(), P("dp", None, None, "space"))
    return jax.shard_map(
        local,
        mesh=mesh,
        in_specs=placed,
        out_specs=(P("dp", None, None, "space"), P(), P()),
        check_vma=False,
    )
```
